128 devices in a mesh: front: 8 (over x, core), wide: 16 (over z, y).
Axes of the slice: x: 4, y: 4, z: 4, core: 2. Of those that a mesh axis runs over, the one named last changes fastest.
Arguments:
- inv_diag: bfloat16 [8, 8192, 8192], P('front', 'wide'), as said below
- below: bfloat16 [8, 12288, 8192], P('front', 'wide'), may hold values from -0.0625 to 0.0625
- rhs: bfloat16 [8, 8192, 256], P('front', 'wide'), may hold values from -6 to 6
- tile_count: int32 [8], replicated, may hold values from 72 to 96, as said below
- tile_owner: int32 [8, 96, 1], P('front', 'wide'), may hold values from 0 to 7; in each aligned block of 6 rows (0 to 5, 6 to 11, ..., all dimensions but the last counted through in order) at most 2 rows name the same one
- tile_rows: int32 [8, 96, 128], P('front', 'wide'), may hold values from 0 to 511
- parent_rhs: bfloat16 [8, 8192, 256], P('front', 'wide'), may hold values from -6 to 6
Outputs:
- solved: bfloat16 [8, 8192, 256], P('front', 'wide')
- parent_new: float32 [8, 8192, 256], P('front', 'wide')
The draws below stay inside these ranges and needn't reach their ends.
Inputs may be any that keep to these rules, and one draw needn't show every extreme that they name: Each inv_diag[f] is lower triangular. Tiles of front f with index at least tile_count[f] carry nothing; some front has all 96 tiles live. `tile_owner`: among the 6 tiles of one device (aligned blocks of tiles), no front index is named more than 2 times.
All inputs are finite; a program needn't handle non-finite values.
Results may differ from the reference program's by a relative error of at most 0.0037.
Values may be sent and summed in bfloat16 or wider, within the bound.
A program may use at most 128 MiB of HBM per device.

```python
import math
import jax
import jax.numpy as jnp
import numpy as np
from jax import lax

PIVOTS = 8192
RHS_COLS = 256
TILE_ROWS = 128
CAPACITY = 2
PARENT_DEV = 512
FRONTS = 8
TILES_DEV = 6
BELOW = 12288
TILES = 96
PARENT = 8192


def draw_inv_diag(key, part):
    first, second = jax.random.split(key)
    lower = jax.random.normal(first, (FRONTS, PIVOTS, PIVOTS), jnp.float32)
    lower = lower * (1.5 / PIVOTS ** 0.5)
    diagonal = jax.random.uniform(second, (FRONTS, PIVOTS), jnp.float32, 0.5, 1.5)
    row_index = lax.broadcasted_iota(jnp.int32, (PIVOTS, PIVOTS), 0)
    col_index = lax.broadcasted_iota(jnp.int32, (PIVOTS, PIVOTS), 1)
    strict = (row_index > col_index)[None]
    on_diag = (row_index == col_index)[None]
    result = jnp.where(strict, lower, 0.0) + jnp.where(on_diag, diagonal[:, :, None], 0.0)
    return result.astype(jnp.bfloat16)


def draw_tile_count(key, part):
    first, second = jax.random.split(key)
    counts = jax.random.randint(first, (FRONTS,), TILES * 3 // 4, TILES + 1, jnp.int32)
    chosen = jax.random.randint(second, (), 0, FRONTS, jnp.int32)
    return jnp.where(jnp.arange(FRONTS, dtype=jnp.int32) == chosen, TILES, counts).astype(jnp.int32)


def with_ends(values, own_key, least, high):
    place = [jax.random.randint(jax.random.fold_in(own_key, axis), (), 0, length) for axis, length in enumerate(values.shape)]
    main_axis = values.shape.index(max(values.shape))
    next_to = place[:main_axis] + [(place[main_axis] + 1) % values.shape[main_axis]] + place[main_axis + 1:]
    return values.at[tuple(place)].set(least).at[tuple(next_to)].set(high)


def levels(key, shape, cuts, least, largest):
    def one(position, blocks):
        draws = jax.random.uniform(jax.random.fold_in(jax.random.fold_in(key, 6), position), (blocks,), jnp.float32, least / len(cuts), largest / len(cuts))
        return jnp.repeat(jnp.exp(draws), shape[position] // blocks).reshape((-1,) + (1,) * (len(shape) - position - 1))

    factor_of = one(*cuts[0])
    for cut in cuts[1:]:
        factor_of = factor_of * one(*cut)
    return factor_of


def routed_block(own_key, own, number, rows, amount, top, limit, skew):
    sequence = jax.random.permutation(own_key, amount)
    crowded, usual = shares(amount, rows * top, limit, skew, True), shares(amount, rows * top, limit, skew, False)
    places = jnp.arange(amount)

    def named(sizes, offset_by):
        used = int((sizes > 0).sum())
        fixed = max(1, used // 4)
        passed = fixed + (places - fixed + offset_by * (used - fixed)) % max(1, amount - fixed)
        return jnp.zeros((amount,), jnp.int32).at[sequence[jnp.where(places < fixed, places, passed)]].set(jnp.asarray(sizes, jnp.int32))

    sizes = jnp.where(number % 4 == 0, named(crowded, number // 4), named(usual, number - number // 4 - 1))
    mixed = jax.random.permutation(jax.random.fold_in(own, 3), amount)
    giver, receiver = mixed[0:amount // 2 * 2:2], mixed[1:amount // 2 * 2:2]
    margin = jnp.minimum(sizes[giver] - 1, limit - sizes[receiver]) // 2
    margin = jnp.where((giver == sequence[0]) | (receiver == sequence[0]) | (sizes[receiver] == 0), 0, jnp.maximum(margin, 0))
    passed = jax.random.randint(jax.random.fold_in(own, 4), (amount // 2,), 0, 1 << 20) % (margin + 1)
    sizes = sizes.at[giver].add(-passed).at[receiver].add(passed)
    items = jnp.searchsorted(jnp.cumsum(sizes), jnp.arange(rows * top), side="right").astype(jnp.int32)
    table = items.reshape(top, rows).T
    table = table[jax.random.permutation(jax.random.fold_in(own, 1), rows)]
    offset_by = jax.random.randint(jax.random.fold_in(own, 2), (rows, 1), 0, top)
    return jnp.take_along_axis(table, (jnp.arange(top)[None, :] + offset_by) % top, axis=1)


def shares(amount, total, bound, slope, full):
    loads = [(1 << 20) // math.isqrt(grade ** slope) + 1 for grade in range(1, amount + 1)]
    largest = bound if full else min(bound, max(-(-total // amount), total * loads[0] // sum(loads)))
    least = 1 if total - largest >= amount - 1 else 0
    given, surplus = [largest] + [least] * (amount - 1), total - largest - least * (amount - 1)
    while surplus > 0:
        free = [i for i in range(1, amount) if given[i] < largest] or [i for i in range(1, amount) if given[i] < bound]
        whole, budget = sum([loads[i] for i in free]), surplus
        for i in free:
            extra = min(bound - given[i], max(1, budget * loads[i] // whole), surplus)
            given[i] = given[i] + extra
            surplus = surplus - extra
    return np.array(given)


def noise(key, extent, spread, most, cuts=(), held_as=jnp.bfloat16):
    gain = levels(key, extent, cuts, -0.22, 0.18) if cuts else 1.0
    values = jax.random.normal(key, extent, jnp.float32) * spread * gain
    return jnp.minimum(jnp.maximum(values, -most), most).astype(held_as)


def setup_inputs(seed: int = 0) -> dict:
    streams_of = jax.random.split(jax.random.key(seed), 8)
    inv_diag = draw_inv_diag(jax.random.fold_in(streams_of[7], 71), 0)
    below = noise(streams_of[1], (FRONTS, BELOW, PIVOTS), PIVOTS ** -0.5, 0.0625, ((0, 8), (1, 16)))
    rhs = noise(streams_of[2], (FRONTS, PIVOTS, RHS_COLS), 1.0, 6.0, ((0, 8), (1, 16)))
    tile_count = draw_tile_count(jax.random.fold_in(streams_of[7], 71), 0)
    tile_owner_keys = jax.random.split(jax.random.fold_in(streams_of[4], 1), FRONTS * TILES // TILES_DEV)
    tile_owner_turns = jax.random.permutation(jax.random.fold_in(streams_of[4], 3), FRONTS * TILES // TILES_DEV)
    tile_owner = jax.vmap(lambda own, number: routed_block(jax.random.fold_in(streams_of[4], 2), own, number, TILES_DEV, FRONTS, 1, CAPACITY, 2))(tile_owner_keys, tile_owner_turns).reshape((FRONTS, TILES, 1))
    tile_rows = with_ends(jax.random.randint(streams_of[5], (FRONTS, TILES, TILE_ROWS), 0, PARENT_DEV), jax.random.fold_in(streams_of[5], 1), 0, PARENT_DEV - 1).astype(jnp.int32)
    parent_rhs = noise(streams_of[6], (FRONTS, PARENT, RHS_COLS), 1.0, 6.0, ((0, 8), (1, 16)))
    return {"inv_diag": inv_diag, "below": below, "rhs": rhs, "tile_count": tile_count, "tile_owner": tile_owner, "tile_rows": tile_rows, "parent_rhs": parent_rhs}


def reference(inv_diag, below, rhs, tile_count, tile_owner, tile_rows, parent_rhs):
    def per_front(front_number):
        solved_one = jnp.dot(inv_diag[front_number], rhs[front_number], preferred_element_type=jnp.float32).astype(jnp.bfloat16)
        update_one = jnp.dot(below[front_number], solved_one, preferred_element_type=jnp.float32).astype(jnp.bfloat16)
        return solved_one, update_one

    solved, updates = lax.map(per_front, jnp.arange(FRONTS, dtype=jnp.int32))
    living = jnp.arange(TILES, dtype=jnp.int32)[None, :] < tile_count[:, None]
    update_tiles = updates.reshape(FRONTS, TILES, TILE_ROWS, RHS_COLS)
    update_tiles = jnp.where(living[:, :, None, None], update_tiles, jnp.zeros_like(update_tiles))
    owners = tile_owner[:, :, 0]
    wide_slot = (jnp.arange(TILES, dtype=jnp.int32) // TILES_DEV)[None, :]
    flat_index = (owners * PARENT + wide_slot * PARENT_DEV)[:, :, None] + tile_rows
    parent_sum = parent_rhs.astype(jnp.float32).reshape(FRONTS * PARENT, RHS_COLS)
    parent_sum = parent_sum.at[flat_index.reshape(-1).astype(jnp.int32)].add(-update_tiles.astype(jnp.float32).reshape(-1, RHS_COLS))
    return solved, parent_sum.reshape(FRONTS, PARENT, RHS_COLS)
```

```python
import functools

import jax
import jax.numpy as jnp
from jax import lax
from jax.experimental import pallas as pl
from jax.experimental.pallas import tpu as pltpu
from jax.sharding import PartitionSpec as P

MESH = pl.DeviceIdType.MESH
CHUNK = 128
PLUS, MINUS = 1, -1
DIRS = [(a, s) for a in (0, 1) for s in (PLUS, MINUS)]
D1, R1, OWN, NEAR_M, NEAR_P, OPP_A, OPP_B, R_OWN, R_NEAR_M, R_NEAR_P, R_OPP = range(11)
PER_LINK = 11


def kernel(
    inv_hbm, below_hbm, rhs_hbm, parent_hbm, rows_ref, owner_ref, count_ref,
    solved_hbm, parent_out_hbm,
    inv, below, rbuf, sbuf, s_acc, u_acc, u_tiles, slot_idx,
    rows_out, rows_in, packed, arrived, relayed, hits, parent, parent_out,
    g_send, g_recv, x_send, x_recv, r_send, r_recv, loc, out_sem,
):
    f = lax.axis_index("front")
    w = lax.axis_index("wide")
    z, y = w // 4, w % 4
    chip, core = f // 2, f % 2
    pb = rbuf.shape[1] // 16
    half, quarter = pb // 2, pb // 4
    tiles, height = u_tiles.shape[0], u_tiles.shape[1]
    slots = arrived.shape[2]
    parent_rows = parent.shape[0]
    chunks = rbuf.shape[0]
    bufs = [rbuf.at[c] for c in range(chunks)] + [sbuf.at[c] for c in range(chunks)]
    sends = []

    def wide_of(off):
        return ((z + off[1] + 4) % 4) * 4 + (y + off[0] + 4) % 4

    def vec(axis, k):
        return (k, 0) if axis == 0 else (0, k)

    def add(p, q):
        return (p[0] + q[0], p[1] + q[1])

    def region(g, off, h, q=None):
        start = wide_of(off) * pb + h * half + (0 if q is None else q * quarter)
        size = half if q is None else quarter
        return bufs[g].at[pl.ds(pl.multiple_of(start, quarter), size)]

    def gcopy(g, axis, s, msg, ref):
        i = (axis * 2 + (0 if s == PLUS else 1)) * PER_LINK + msg
        return pltpu.make_async_remote_copy(
            src_ref=ref, dst_ref=ref, send_sem=g_send.at[g, i], recv_sem=g_recv.at[g, i],
            device_id=(f, wide_of(vec(axis, s))), device_id_type=MESH,
        )

    def gsend(g, axis, s, msg, ref):
        copy = gcopy(g, axis, s, msg, ref)
        copy.start()
        sends.append(copy)

    def gwait(g, axis, s, msg, ref):
        gcopy(g, axis, s, msg, ref).wait_recv()

    def quart(s):
        return 0 if s == PLUS else 1

    here = (0, 0)

    def g_own(g):
        for axis, s in DIRS:
            gsend(g, axis, s, D1, region(g, here, axis))
        for axis, s in DIRS:
            gsend(g, axis, s, OWN, region(g, here, 1 - axis))

    def g_d1(g):
        for axis, s in DIRS:
            off = vec(axis, -s)
            gwait(g, axis, s, D1, region(g, off, axis))
            gsend(g, axis, s, R1, region(g, off, axis, quart(s)))
            for t in (PLUS, MINUS):
                gsend(g, 1 - axis, t, NEAR_M if s == PLUS else NEAR_P, region(g, off, axis))

    def g_r1(g):
        for axis, s in DIRS:
            ref = region(g, vec(axis, 2), axis, quart(s))
            gwait(g, axis, s, R1, ref)
            for t in (PLUS, MINUS):
                gsend(g, 1 - axis, t, OPP_A if s == PLUS else OPP_B, ref)

    def g_d2own(g):
        for axis, s in DIRS:
            off = vec(axis, -s)
            gwait(g, axis, s, OWN, region(g, off, 1 - axis))
            gsend(g, axis, s, R_OWN, region(g, off, 1 - axis, quart(s)))

    def g_d2near(g):
        for j, msg, relay in ((MINUS, NEAR_M, R_NEAR_M), (PLUS, NEAR_P, R_NEAR_P)):
            for axis, s in DIRS:
                off = add(vec(axis, -s), vec(1 - axis, j))
                gwait(g, axis, s, msg, region(g, off, 1 - axis))
                gsend(g, axis, s, relay, region(g, off, 1 - axis, quart(s)))

    def g_d2opp(g):
        for axis, s in DIRS:
            off = add(vec(axis, -s), vec(1 - axis, 2))
            for q, msg in ((0, OPP_A), (1, OPP_B)):
                ref = region(g, off, 1 - axis, q)
                gwait(g, axis, s, msg, ref)
                if q == quart(s):
                    gsend(g, axis, s, R_OPP, ref)

    def g_r2(g, msg, j):
        for axis, s in DIRS:
            off = add(vec(axis, 2), vec(1 - axis, j))
            gwait(g, axis, s, msg, region(g, off, 1 - axis, quart(s)))

    def g_r2all(g):
        for msg, j in ((R_OWN, 0), (R_NEAR_M, MINUS), (R_NEAR_P, PLUS), (R_OPP, 2)):
            g_r2(g, msg, j)

    own = pl.ds(pl.multiple_of(w * pb, pb), pb)
    loads = []
    for c in range(chunks):
        cols = pl.ds(c * CHUNK, CHUNK)
        loads.append(pltpu.make_async_copy(rhs_hbm.at[:, cols], rbuf.at[c, own], loc.at[c]))
    loads.append(pltpu.make_async_copy(inv_hbm, inv, loc.at[chunks]))
    loads.append(pltpu.make_async_copy(below_hbm, below, loc.at[chunks + 1]))
    loads.append(pltpu.make_async_copy(parent_hbm, parent, loc.at[chunks + 2]))
    for copy in loads:
        copy.start()

    barrier = pltpu.get_barrier_semaphore()
    for axis, s in DIRS:
        pl.semaphore_signal(barrier, inc=1, device_id=(f, wide_of(vec(axis, s))), device_id_type=MESH)
    for d in range(1, 8):
        pl.semaphore_signal(barrier, inc=1, device_id=((f + d) % 8, w), device_id_type=MESH)
    pl.semaphore_wait(barrier, 11)

    loads[0].wait()
    g_own(0)

    live = [w * tiles + j < count_ref[f] for j in range(tiles)]
    none = jnp.full((1, height), parent_rows, jnp.int32)
    rows_out[...] = jnp.full(rows_out.shape, parent_rows, jnp.int32)
    for g in range(8):
        index = [jnp.int32(0)] * slots
        found = [jnp.int32(0)] * slots
        seen = jnp.int32(0)
        for j in range(tiles):
            hit = owner_ref[j] == g
            for k in range(slots):
                this = jnp.logical_and(hit, seen == k)
                index[k] = jnp.where(this, j, index[k])
                found[k] = jnp.where(jnp.logical_and(this, live[j]), 1, found[k])
            seen = seen + jnp.where(hit, 1, 0)
        for k in range(slots):
            slot_idx[g * slots + k] = index[k]
            rows_out[g, k:k + 1, :] = jnp.where(found[k] == 1, rows_ref[pl.ds(index[k], 1), :], none)
    rows_in[f] = rows_out[f]
    rcopies = []
    for d in range(1, 8):
        to = (f + d) % 8
        copy = pltpu.make_async_remote_copy(
            src_ref=rows_out.at[to], dst_ref=rows_in.at[f], send_sem=r_send.at[d], recv_sem=r_recv.at[d],
            device_id=(to, w), device_id_type=MESH,
        )
        copy.start()
        sends.append(copy)

    def wait_rows():
        for d in range(1, 8):
            pltpu.make_async_remote_copy(
                src_ref=rows_in.at[(f + 8 - d) % 8], dst_ref=rows_in.at[(f + 8 - d) % 8],
                send_sem=r_send.at[d], recv_sem=r_recv.at[d], device_id=((f + d) % 8, w), device_id_type=MESH,
            ).wait_recv()

    def build_hits():
        position = lax.broadcasted_iota(jnp.int32, (parent_rows, height), 0)

        def one(i, carry):
            for k in range(slots):
                row = rows_in[i, k:k + 1, :]
                at = pl.ds(pl.multiple_of((i * slots + k) * height, height), height)
                hits[:, at] = jnp.where(position == row, 1.0, 0.0).astype(jnp.bfloat16)
            return carry

        lax.fori_loop(0, 8, one, 0)

    def block(ref, acc, src, k):
        at = pl.ds(pl.multiple_of(k * pb, pb), pb)
        acc[...] += jnp.dot(ref[:, at], src[at, :], preferred_element_type=jnp.float32)

    def mm(ref, acc, src, lo, hi, place=lambda i: i):
        def step(i, carry):
            block(ref, acc, src, place(i))
            return carry

        lax.fori_loop(lo, hi, step, 0)

    def store_solved(c):
        sbuf[c, own, :] = s_acc[...].astype(jnp.bfloat16)

    def solved_out(c):
        copy = pltpu.make_async_copy(sbuf.at[c, own], solved_hbm.at[:, pl.ds(c * CHUNK, CHUNK)], out_sem.at[c])
        copy.start()
        return copy

    def xcopy(c, sid, rid, src, dst, to):
        return pltpu.make_async_remote_copy(
            src_ref=src, dst_ref=dst, send_sem=x_send.at[c, sid], recv_sem=x_recv.at[c, rid],
            device_id=(to, w), device_id_type=MESH,
        )

    def xstart(*args):
        copy = xcopy(*args)
        copy.start()
        sends.append(copy)

    def chip_at(k):
        return (chip + k + 4) % 4

    def pack(c):
        for j in range(tiles):
            value = u_acc[j * height:(j + 1) * height, :]
            u_tiles[j] = jnp.where(live[j], value, jnp.zeros_like(value)).astype(jnp.bfloat16)

        def one(i, carry):
            for k in range(slots):
                packed[c, i, k] = u_tiles[slot_idx[i * slots + k]]
            return carry

        lax.fori_loop(0, 8, one, 0)
        for k in range(slots):
            arrived[c, f, k] = packed[c, f, k]

    def xsend(c):
        for n, s in enumerate((PLUS, MINUS)):
            for c2 in range(2):
                to = chip_at(2) * 2 + c2
                xstart(c, 5 + n * 2 + c2, 5 + n * 2 + c2, packed.at[c, to, n], relayed.at[c, n, c2], chip_at(s) * 2 + core)
        for n, s in enumerate((PLUS, MINUS)):
            for c2 in range(2):
                to = chip_at(s) * 2 + c2
                xstart(c, 1 + n * 2 + c2, 1 + n * 2 + core, packed.at[c, to], arrived.at[c, f], to)
        to = chip * 2 + 1 - core
        xstart(c, 0, 0, packed.at[c, to], arrived.at[c, f], to)

    def xrelay(c):
        for n, s in enumerate((PLUS, MINUS)):
            for c2 in range(2):
                ref = relayed.at[c, n, c2]
                xcopy(c, 5 + n * 2 + c2, 5 + n * 2 + c2, ref, ref, chip_at(s) * 2 + core).wait_recv()
                source = chip_at(-s) * 2 + core
                xstart(c, 9 + n * 2 + c2, 9 + n * 2 + core, ref, arrived.at[c, source, n], chip_at(s) * 2 + c2)

    def xwait(c):
        other = chip * 2 + 1 - core
        ref = arrived.at[c, other]
        xcopy(c, 0, 0, ref, ref, other).wait_recv()
        for n, s in enumerate((PLUS, MINUS)):
            for c2 in range(2):
                ref = arrived.at[c, chip_at(-s) * 2 + c2]
                xcopy(c, 0, 1 + n * 2 + c2, ref, ref, other).wait_recv()
        for n, s in enumerate((PLUS, MINUS)):
            for c2 in range(2):
                ref = arrived.at[c, chip_at(2) * 2 + c2, n]
                xcopy(c, 0, 9 + n * 2 + c2, ref, ref, other).wait_recv()

    def scatter(c):
        cols = slice(c * CHUNK, (c + 1) * CHUNK)
        per = 4 * slots * height

        def step(i, acc):
            at = pl.ds(pl.multiple_of(i * per, per), per)
            values = arrived[c, pl.ds(i * 4, 4)].reshape(per, CHUNK)
            return acc - jnp.dot(hits[:, at], values, preferred_element_type=jnp.float32)

        parent_out[c] = parent[:, cols].astype(jnp.float32)
        for i in range(2):
            parent_out[c] = step(i, parent_out[c])
        copy = pltpu.make_async_copy(parent_out.at[c], parent_out_hbm.at[:, pl.ds(c * CHUNK, CHUNK)], out_sem.at[chunks + c])
        copy.start()
        return copy

    nb = 16
    R, S = (0, 1), (2, 3)
    g_d1(0)
    g_r1(0)
    loads[1].wait()
    g_own(1)
    g_d2own(0)
    g_d2near(0)
    g_d2opp(0)
    g_d1(1)
    g_r2all(0)
    g_r1(1)
    loads[2].wait()
    s_acc[...] = jnp.zeros_like(s_acc)
    mm(inv, s_acc, rbuf.at[0], 0, 5)
    g_d2own(1)
    mm(inv, s_acc, rbuf.at[0], 5, 11)
    g_d2near(1)
    mm(inv, s_acc, rbuf.at[0], 11, nb)
    store_solved(0)
    g_own(2)
    g_d2opp(1)
    outs = [solved_out(0)]
    g_d1(2)
    g_r2all(1)
    g_r1(2)
    s_acc[...] = jnp.zeros_like(s_acc)
    mm(inv, s_acc, rbuf.at[1], 0, 5)
    g_d2own(2)
    mm(inv, s_acc, rbuf.at[1], 5, 11)
    g_d2near(2)
    mm(inv, s_acc, rbuf.at[1], 11, nb)
    store_solved(1)
    g_own(3)
    g_d2opp(2)
    outs.append(solved_out(1))
    wait_rows()
    g_d1(3)
    g_r2all(2)
    g_r1(3)
    loads[3].wait()
    u_acc[...] = jnp.zeros_like(u_acc)
    mm(below, u_acc, sbuf.at[0], 0, 5)
    g_d2own(3)
    mm(below, u_acc, sbuf.at[0], 5, 11)
    g_d2near(3)
    mm(below, u_acc, sbuf.at[0], 11, nb)
    pack(0)
    xsend(0)
    g_d2opp(3)
    u_acc[...] = jnp.zeros_like(u_acc)
    src = sbuf.at[1]
    mm(below, u_acc, src, 0, 1, lambda i: w)
    mm(below, u_acc, src, 0, 4, lambda i: wide_of(((2 * (i % 2) - 1) * (1 - i // 2), (2 * (i % 2) - 1) * (i // 2))))
    xrelay(0)
    mm(below, u_acc, src, 0, 4, lambda i: wide_of((2 * (i % 2) - 1, 2 * (i // 2) - 1)))
    build_hits()
    g_r2(3, R_OWN, 0)
    mm(below, u_acc, src, 0, 2, lambda i: wide_of((2 * i, 2 - 2 * i)))
    g_r2(3, R_NEAR_M, MINUS)
    g_r2(3, R_NEAR_P, PLUS)
    mm(below, u_acc, src, 0, 4, lambda i: wide_of((
        2 * (1 - i // 2) + (2 * (i % 2) - 1) * (i // 2), (2 * (i % 2) - 1) * (1 - i // 2) + 2 * (i // 2))))
    g_r2(3, R_OPP, 2)
    mm(below, u_acc, src, 0, 1, lambda i: wide_of((2, 2)))
    pack(1)
    xsend(1)
    xwait(0)
    loads[4].wait()
    outs.append(scatter(0))
    xrelay(1)
    xwait(1)
    outs.append(scatter(1))
    for copy in sends:
        copy.wait_send()
    for copy in outs:
        copy.wait()


def call(inv, below, rhs, parent_rhs, tile_rows, owners, tile_count):
    rows, pivots = inv.shape
    under = below.shape[0]
    width = rhs.shape[1]
    chunks = width // CHUNK
    tiles, height = tile_rows.shape
    slots = 2
    parent_rows = parent_rhs.shape[0]
    bf, f32 = jnp.bfloat16, jnp.float32
    anyspace = pl.BlockSpec(memory_space=pl.ANY)
    vmem = pl.BlockSpec(memory_space=pltpu.VMEM)
    smem = pl.BlockSpec(memory_space=pltpu.SMEM)
    dma = pltpu.SemaphoreType.DMA
    return pl.pallas_call(
        kernel,
        out_shape=(
            jax.ShapeDtypeStruct((rows, width), bf),
            jax.ShapeDtypeStruct((parent_rows, width), f32),
        ),
        in_specs=[anyspace] * 4 + [vmem, smem, smem],
        out_specs=(anyspace, anyspace),
        scratch_shapes=[
            pltpu.VMEM((rows, pivots), bf),
            pltpu.VMEM((under, pivots), bf),
            pltpu.VMEM((chunks, pivots, CHUNK), bf),
            pltpu.VMEM((chunks, pivots, CHUNK), bf),
            pltpu.VMEM((rows, CHUNK), f32),
            pltpu.VMEM((under, CHUNK), f32),
            pltpu.VMEM((tiles, height, CHUNK), bf),
            pltpu.SMEM((8 * slots,), jnp.int32),
            pltpu.VMEM((8, 8, height), jnp.int32),
            pltpu.VMEM((8, 8, height), jnp.int32),
            pltpu.VMEM((chunks, 8, slots, height, CHUNK), bf),
            pltpu.VMEM((chunks, 8, slots, height, CHUNK), bf),
            pltpu.VMEM((chunks, 2, 2, height, CHUNK), bf),
            pltpu.VMEM((parent_rows, 8 * slots * height), bf),
            pltpu.VMEM((parent_rows, width), bf),
            pltpu.VMEM((chunks, parent_rows, CHUNK), f32),
            dma((2 * chunks, 4 * PER_LINK)),
            dma((2 * chunks, 4 * PER_LINK)),
            dma((chunks, 13)),
            dma((chunks, 13)),
            dma((8,)),
            dma((8,)),
            dma((chunks + 3,)),
            dma((2 * chunks,)),
        ],
        compiler_params=pltpu.CompilerParams(
            collective_id=0, has_side_effects=True, vmem_limit_bytes=60 * 1024 * 1024
        ),
        name="solve_extend_add",
    )(inv, below, rhs, parent_rhs, tile_rows, owners, tile_count)


def body(inv_diag, below, rhs, tile_count, tile_owner, tile_rows, parent_rhs):
    solved, parent_new = call(
        inv_diag[0], below[0], rhs[0], parent_rhs[0], tile_rows[0], tile_owner[0, :, 0], tile_count
    )
    return solved[None], parent_new[None]


def solution(mesh):
    spec = P("front", "wide", None)
    return jax.shard_map(
        body,
        mesh=mesh,
        in_specs=(spec, spec, spec, P(), spec, spec, spec),
        out_specs=(spec, spec),
        check_vma=False,
    )
```

```python
import functools

import jax
import jax.numpy as jnp
from jax import lax
from jax.experimental import pallas as pl
from jax.experimental.pallas import tpu as pltpu
from jax.sharding import PartitionSpec as P

MESH = pl.DeviceIdType.MESH
CHUNK = 128
PLUS, MINUS = 1, -1
DIRS = [(a, s) for a in (0, 1) for s in (PLUS, MINUS)]
D1, R1, OWN, NEAR_M, NEAR_P, OPP_A, OPP_B, R_OWN, R_NEAR_M, R_NEAR_P, R_OPP = range(11)
PER_LINK = 11


def kernel(
    inv_hbm, below_hbm, rhs_hbm, parent_hbm, rows_ref, owner_ref, count_ref,
    solved_out, parent_out,
    inv, below, rbuf, sbuf, s_acc, u_acc, u_tiles, slot_idx,
    rows_out, rows_in, packed, arrived, relayed, hits, parent,
    g_send, g_recv, x_send, x_recv, r_send, r_recv, loc,
):
    f = lax.axis_index("front")
    w = lax.axis_index("wide")
    z, y = w // 4, w % 4
    chip, core = f // 2, f % 2
    pb = rbuf.shape[1] // 16
    half, quarter = pb // 2, pb // 4
    tiles, height = u_tiles.shape[0], u_tiles.shape[1]
    slots = arrived.shape[2]
    parent_rows = parent.shape[0]
    chunks = rbuf.shape[0]
    bufs = [rbuf.at[c] for c in range(chunks)] + [sbuf.at[c] for c in range(chunks)]
    sends = []

    def wide_of(off):
        return ((z + off[1] + 4) % 4) * 4 + (y + off[0] + 4) % 4

    def vec(axis, k):
        return (k, 0) if axis == 0 else (0, k)

    def add(p, q):
        return (p[0] + q[0], p[1] + q[1])

    def region(g, off, h, q=None):
        start = wide_of(off) * pb + h * half + (0 if q is None else q * quarter)
        size = half if q is None else quarter
        return bufs[g].at[pl.ds(pl.multiple_of(start, quarter), size)]

    def gcopy(g, axis, s, msg, ref):
        i = (axis * 2 + (0 if s == PLUS else 1)) * PER_LINK + msg
        return pltpu.make_async_remote_copy(
            src_ref=ref, dst_ref=ref, send_sem=g_send.at[g, i], recv_sem=g_recv.at[g, i],
            device_id=(f, wide_of(vec(axis, s))), device_id_type=MESH,
        )

    def gsend(g, axis, s, msg, ref):
        copy = gcopy(g, axis, s, msg, ref)
        copy.start()
        sends.append(copy)

    def gwait(g, axis, s, msg, ref):
        gcopy(g, axis, s, msg, ref).wait_recv()

    def quart(s):
        return 0 if s == PLUS else 1

    here = (0, 0)

    def g_own(g):
        for axis, s in DIRS:
            gsend(g, axis, s, D1, region(g, here, axis))
        for axis, s in DIRS:
            gsend(g, axis, s, OWN, region(g, here, 1 - axis))

    def g_d1(g):
        for axis, s in DIRS:
            off = vec(axis, -s)
            gwait(g, axis, s, D1, region(g, off, axis))
            gsend(g, axis, s, R1, region(g, off, axis, quart(s)))
            for t in (PLUS, MINUS):
                gsend(g, 1 - axis, t, NEAR_M if s == PLUS else NEAR_P, region(g, off, axis))

    def g_r1(g):
        for axis, s in DIRS:
            ref = region(g, vec(axis, 2), axis, quart(s))
            gwait(g, axis, s, R1, ref)
            for t in (PLUS, MINUS):
                gsend(g, 1 - axis, t, OPP_A if s == PLUS else OPP_B, ref)

    def g_d2own(g):
        for axis, s in DIRS:
            off = vec(axis, -s)
            gwait(g, axis, s, OWN, region(g, off, 1 - axis))
            gsend(g, axis, s, R_OWN, region(g, off, 1 - axis, quart(s)))

    def g_d2near(g):
        for j, msg, relay in ((MINUS, NEAR_M, R_NEAR_M), (PLUS, NEAR_P, R_NEAR_P)):
            for axis, s in DIRS:
                off = add(vec(axis, -s), vec(1 - axis, j))
                gwait(g, axis, s, msg, region(g, off, 1 - axis))
                gsend(g, axis, s, relay, region(g, off, 1 - axis, quart(s)))

    def g_d2opp(g):
        for axis, s in DIRS:
            off = add(vec(axis, -s), vec(1 - axis, 2))
            for q, msg in ((0, OPP_A), (1, OPP_B)):
                ref = region(g, off, 1 - axis, q)
                gwait(g, axis, s, msg, ref)
                if q == quart(s):
                    gsend(g, axis, s, R_OPP, ref)

    def g_r2(g, msg, j):
        for axis, s in DIRS:
            off = add(vec(axis, 2), vec(1 - axis, j))
            gwait(g, axis, s, msg, region(g, off, 1 - axis, quart(s)))

    def g_r2all(g):
        for msg, j in ((R_OWN, 0), (R_NEAR_M, MINUS), (R_NEAR_P, PLUS), (R_OPP, 2)):
            g_r2(g, msg, j)

    own = pl.ds(pl.multiple_of(w * pb, pb), pb)
    loads = []
    for c in range(chunks):
        cols = pl.ds(c * CHUNK, CHUNK)
        loads.append(pltpu.make_async_copy(rhs_hbm.at[:, cols], rbuf.at[c, own], loc.at[c]))
    loads.append(pltpu.make_async_copy(inv_hbm, inv, loc.at[chunks]))
    loads.append(pltpu.make_async_copy(below_hbm, below, loc.at[chunks + 1]))
    loads.append(pltpu.make_async_copy(parent_hbm, parent, loc.at[chunks + 2]))
    for copy in loads:
        copy.start()

    barrier = pltpu.get_barrier_semaphore()
    for axis, s in DIRS:
        pl.semaphore_signal(barrier, inc=1, device_id=(f, wide_of(vec(axis, s))), device_id_type=MESH)
    for d in range(1, 8):
        pl.semaphore_signal(barrier, inc=1, device_id=((f + d) % 8, w), device_id_type=MESH)
    pl.semaphore_wait(barrier, 11)

    loads[0].wait()
    g_own(0)

    live = [w * tiles + j < count_ref[f] for j in range(tiles)]
    none = jnp.full((1, height), parent_rows, jnp.int32)
    rows_out[...] = jnp.full(rows_out.shape, parent_rows, jnp.int32)
    for g in range(8):
        index = [jnp.int32(0)] * slots
        found = [jnp.int32(0)] * slots
        seen = jnp.int32(0)
        for j in range(tiles):
            hit = owner_ref[j] == g
            for k in range(slots):
                this = jnp.logical_and(hit, seen == k)
                index[k] = jnp.where(this, j, index[k])
                found[k] = jnp.where(jnp.logical_and(this, live[j]), 1, found[k])
            seen = seen + jnp.where(hit, 1, 0)
        for k in range(slots):
            slot_idx[g * slots + k] = index[k]
            rows_out[g, k:k + 1, :] = jnp.where(found[k] == 1, rows_ref[index[k]], none)
    rows_in[f] = rows_out[f]
    rcopies = []
    for d in range(1, 8):
        to = (f + d) % 8
        copy = pltpu.make_async_remote_copy(
            src_ref=rows_out.at[to], dst_ref=rows_in.at[f], send_sem=r_send.at[d], recv_sem=r_recv.at[d],
            device_id=(to, w), device_id_type=MESH,
        )
        copy.start()
        sends.append(copy)

    def wait_rows():
        for d in range(1, 8):
            pltpu.make_async_remote_copy(
                src_ref=rows_in.at[(f + 8 - d) % 8], dst_ref=rows_in.at[(f + 8 - d) % 8],
                send_sem=r_send.at[d], recv_sem=r_recv.at[d], device_id=((f + d) % 8, w), device_id_type=MESH,
            ).wait_recv()

    def build_hits():
        position = lax.broadcasted_iota(jnp.int32, (parent_rows, height), 0)

        def one(i, carry):
            for k in range(slots):
                row = rows_in[i, k:k + 1, :]
                at = pl.ds(pl.multiple_of((i * slots + k) * height, height), height)
                hits[:, at] = jnp.where(position == row, 1.0, 0.0).astype(jnp.bfloat16)
            return carry

        lax.fori_loop(0, 8, one, 0)

    def block(ref, acc, src, k):
        at = pl.ds(pl.multiple_of(k * pb, pb), pb)
        acc[...] += jnp.dot(ref[:, at], src[at, :], preferred_element_type=jnp.float32)

    def mm(ref, acc, src, lo, hi, place=lambda i: i):
        def step(i, carry):
            block(ref, acc, src, place(i))
            return carry

        lax.fori_loop(lo, hi, step, 0)

    def xcopy(c, sid, rid, src, dst, to):
        return pltpu.make_async_remote_copy(
            src_ref=src, dst_ref=dst, send_sem=x_send.at[c, sid], recv_sem=x_recv.at[c, rid],
            device_id=(to, w), device_id_type=MESH,
        )

    def xstart(*args):
        copy = xcopy(*args)
        copy.start()
        sends.append(copy)

    def chip_at(k):
        return (chip + k + 4) % 4

    def pack(c):
        for j in range(tiles):
            value = u_acc[j * height:(j + 1) * height, :]
            u_tiles[j] = jnp.where(live[j], value, jnp.zeros_like(value)).astype(jnp.bfloat16)

        def one(i, carry):
            for k in range(slots):
                packed[c, i, k] = u_tiles[slot_idx[i * slots + k]]
            return carry

        lax.fori_loop(0, 8, one, 0)
        for k in range(slots):
            arrived[c, f, k] = packed[c, f, k]

    def xsend(c):
        for n, s in enumerate((PLUS, MINUS)):
            for c2 in range(2):
                to = chip_at(2) * 2 + c2
                xstart(c, 5 + n * 2 + c2, 5 + n * 2 + c2, packed.at[c, to, n], relayed.at[c, n, c2], chip_at(s) * 2 + core)
        for n, s in enumerate((PLUS, MINUS)):
            for c2 in range(2):
                to = chip_at(s) * 2 + c2
                xstart(c, 1 + n * 2 + c2, 1 + n * 2 + core, packed.at[c, to], arrived.at[c, f], to)
        to = chip * 2 + 1 - core
        xstart(c, 0, 0, packed.at[c, to], arrived.at[c, f], to)

    def xrelay(c):
        for n, s in enumerate((PLUS, MINUS)):
            for c2 in range(2):
                ref = relayed.at[c, n, c2]
                xcopy(c, 5 + n * 2 + c2, 5 + n * 2 + c2, ref, ref, chip_at(s) * 2 + core).wait_recv()
                source = chip_at(-s) * 2 + core
                xstart(c, 9 + n * 2 + c2, 9 + n * 2 + core, ref, arrived.at[c, source, n], chip_at(s) * 2 + c2)

    def xwait(c):
        other = chip * 2 + 1 - core
        ref = arrived.at[c, other]
        xcopy(c, 0, 0, ref, ref, other).wait_recv()
        for n, s in enumerate((PLUS, MINUS)):
            for c2 in range(2):
                ref = arrived.at[c, chip_at(-s) * 2 + c2]
                xcopy(c, 0, 1 + n * 2 + c2, ref, ref, other).wait_recv()
        for n, s in enumerate((PLUS, MINUS)):
            for c2 in range(2):
                ref = arrived.at[c, chip_at(2) * 2 + c2, n]
                xcopy(c, 0, 9 + n * 2 + c2, ref, ref, other).wait_recv()

    def scatter(c):
        cols = slice(c * CHUNK, (c + 1) * CHUNK)
        per = 4 * slots * height

        def step(i, acc):
            at = pl.ds(pl.multiple_of(i * per, per), per)
            values = arrived[c, pl.ds(i * 4, 4)].reshape(per, CHUNK)
            return acc - jnp.dot(hits[:, at], values, preferred_element_type=jnp.float32)

        parent_out[:, cols] = step(1, step(0, parent[:, cols].astype(jnp.float32)))

    def sign(i):
        return 2 * (i % 2) - 1

    def at_near(i):
        return wide_of((sign(i) * (1 - i // 2), sign(i) * (i // 2)))

    def at_diagonal(i):
        return wide_of((sign(i), 2 * (i // 2) - 1))

    def at_far(i):
        return wide_of((2 * i, 2 - 2 * i))

    def at_farther(i):
        return wide_of((2 * (1 - i // 2) + sign(i) * (i // 2), sign(i) * (1 - i // 2) + 2 * (i // 2)))

    sides = [(inv, s_acc)] * chunks + [(below, u_acc)] * chunks

    def take(g, count, place):
        mm(sides[g][0], sides[g][1], bufs[g], 0, count, place)

    def take_own(g):
        acc = sides[g][1]
        acc[...] = jnp.zeros_like(acc)
        take(g, 1, lambda i: w)

    def middle(g):
        take_own(g)
        g_d2own(g)
        take(g, 4, at_near)
        g_d2near(g)

    def late_first(g):
        g_r2(g, R_OWN, 0)
        take(g, 2, at_far)

    def late_last(g):
        g_r2(g, R_NEAR_M, MINUS)
        g_r2(g, R_NEAR_P, PLUS)
        take(g, 4, at_farther)
        g_r2(g, R_OPP, 2)
        take(g, 1, lambda i: wide_of((2, 2)))

    def store_solved(c):
        value = s_acc[...].astype(jnp.bfloat16)
        sbuf[c, own, :] = value
        solved_out[:, c * CHUNK:(c + 1) * CHUNK] = value

    g_d1(0)
    g_r1(0)
    loads[1].wait()
    loads[2].wait()
    middle(0)
    g_own(1)
    take(0, 4, at_diagonal)
    g_d2opp(0)
    wait_rows()
    build_hits()
    g_d1(1)
    late_first(0)
    g_r1(1)
    late_last(0)
    store_solved(0)
    middle(1)
    g_own(2)
    take(1, 4, at_diagonal)
    g_d2opp(1)
    g_d1(2)
    late_first(1)
    g_r1(2)
    late_last(1)
    store_solved(1)
    loads[3].wait()
    middle(2)
    g_own(3)
    take(2, 4, at_diagonal)
    g_d2opp(2)
    g_d1(3)
    late_first(2)
    g_r1(3)
    late_last(2)
    pack(0)
    xsend(0)
    middle(3)
    xrelay(0)
    take(3, 4, at_diagonal)
    g_d2opp(3)
    late_first(3)
    late_last(3)
    pack(1)
    xsend(1)
    loads[4].wait()
    xwait(0)
    scatter(0)
    xrelay(1)
    xwait(1)
    scatter(1)
    for copy in sends:
        copy.wait_send()


def write_kernel(solved_in, parent_in, solved_hbm, parent_hbm, sem):
    copies = [
        pltpu.make_async_copy(solved_in, solved_hbm, sem.at[0]),
        pltpu.make_async_copy(parent_in, parent_hbm, sem.at[1]),
    ]
    for copy in copies:
        copy.start()
    for copy in copies:
        copy.wait()


def call(inv, below, rhs, parent_rhs, tile_rows, owners, tile_count):
    rows, pivots = inv.shape
    under = below.shape[0]
    width = rhs.shape[1]
    chunks = width // CHUNK
    tiles, _, height = tile_rows.shape
    slots = 2
    parent_rows = parent_rhs.shape[0]
    bf, f32 = jnp.bfloat16, jnp.float32
    anyspace = pl.BlockSpec(memory_space=pl.ANY)
    hbm = pl.BlockSpec(memory_space=pltpu.HBM)
    vmem = pl.BlockSpec(memory_space=pltpu.VMEM)
    smem = pl.BlockSpec(memory_space=pltpu.SMEM)
    dma = pltpu.SemaphoreType.DMA
    solved, parent_new = pl.pallas_call(
        kernel,
        out_shape=(
            jax.ShapeDtypeStruct((rows, width), bf),
            jax.ShapeDtypeStruct((parent_rows, width), f32),
        ),
        in_specs=[hbm] * 4 + [vmem, smem, smem],
        out_specs=(vmem, vmem),
        scratch_shapes=[
            pltpu.VMEM((rows, pivots), bf),
            pltpu.VMEM((under, pivots), bf),
            pltpu.VMEM((chunks, pivots, CHUNK), bf),
            pltpu.VMEM((chunks, pivots, CHUNK), bf),
            pltpu.VMEM((rows, CHUNK), f32),
            pltpu.VMEM((under, CHUNK), f32),
            pltpu.VMEM((tiles, height, CHUNK), bf),
            pltpu.SMEM((8 * slots,), jnp.int32),
            pltpu.VMEM((8, 8, height), jnp.int32),
            pltpu.VMEM((8, 8, height), jnp.int32),
            pltpu.VMEM((chunks, 8, slots, height, CHUNK), bf),
            pltpu.VMEM((chunks, 8, slots, height, CHUNK), bf),
            pltpu.VMEM((chunks, 2, 2, height, CHUNK), bf),
            pltpu.VMEM((parent_rows, 8 * slots * height), bf),
            pltpu.VMEM((parent_rows, width), bf),
            dma((2 * chunks, 4 * PER_LINK)),
            dma((2 * chunks, 4 * PER_LINK)),
            dma((chunks, 13)),
            dma((chunks, 13)),
            dma((8,)),
            dma((8,)),
            dma((chunks + 3,)),
        ],
        compiler_params=pltpu.CompilerParams(
            collective_id=0, has_side_effects=True, vmem_limit_bytes=48 * 1024 * 1024
        ),
        name="solve_extend_add",
    )(inv, below, rhs, parent_rhs, tile_rows, owners, tile_count)
    return pl.pallas_call(
        write_kernel,
        out_shape=(
            jax.ShapeDtypeStruct((rows, width), bf),
            jax.ShapeDtypeStruct((parent_rows, width), f32),
        ),
        in_specs=[anyspace] * 2,
        out_specs=(anyspace, anyspace),
        scratch_shapes=[dma((2,))],
        compiler_params=pltpu.CompilerParams(vmem_limit_bytes=1024 * 1024),
        name="write",
    )(solved, parent_new)


def body(inv_diag, below, rhs, tile_count, tile_owner, tile_rows, parent_rhs):
    solved, parent_new = call(
        inv_diag[0], below[0], rhs[0], parent_rhs[0], tile_rows.transpose(1, 0, 2), tile_owner[0, :, 0], tile_count
    )
    return solved[None], parent_new[None]


def solution(mesh):
    spec = P("front", "wide", None)
    return jax.shard_map(
        body,
        mesh=mesh,
        in_specs=(spec, spec, spec, P(), spec, spec, spec),
        out_specs=(spec, spec),
        check_vma=False,
    )
```

```python
import functools

import jax
import jax.numpy as jnp
from jax import lax
from jax.experimental import pallas as pl
from jax.experimental.pallas import tpu as pltpu
from jax.sharding import PartitionSpec as P

MESH = pl.DeviceIdType.MESH
CHUNK = 128
PLUS, MINUS = 1, -1
DIRS = [(a, s) for a in (0, 1) for s in (PLUS, MINUS)]
D1, R1, OWN, NEAR_M, NEAR_P, OPP_A, OPP_B, R_OWN, R_NEAR_M, R_NEAR_P, R_OPP = range(11)
PER_LINK = 11


def kernel(
    inv_hbm, below_hbm, rhs_hbm, parent_hbm, rows_hbm, owner_hbm, count_hbm,
    solved_out, parent_out,
    inv, below, rbuf, sbuf, s_acc, u_acc, u_tiles, slot_idx,
    rows_out, rows_in, packed, arrived, relayed, hits, parent, rows_ref, owner_ref, count_ref,
    g_send, g_recv, x_send, x_recv, r_send, r_recv, loc,
):
    f = lax.axis_index("front")
    w = lax.axis_index("wide")
    z, y = w // 4, w % 4
    chip, core = f // 2, f % 2
    pb = rbuf.shape[1] // 16
    half, quarter = pb // 2, pb // 4
    tiles, height = u_tiles.shape[0], u_tiles.shape[1]
    slots = arrived.shape[2]
    parent_rows = parent.shape[0]
    chunks = rbuf.shape[0]
    bufs = [rbuf.at[c] for c in range(chunks)] + [sbuf.at[c] for c in range(chunks)]
    sends = []

    def wide_of(off):
        return ((z + off[1] + 4) % 4) * 4 + (y + off[0] + 4) % 4

    def vec(axis, k):
        return (k, 0) if axis == 0 else (0, k)

    def add(p, q):
        return (p[0] + q[0], p[1] + q[1])

    def region(g, off, h, q=None):
        start = wide_of(off) * pb + h * half + (0 if q is None else q * quarter)
        size = half if q is None else quarter
        return bufs[g].at[pl.ds(pl.multiple_of(start, quarter), size)]

    def gcopy(g, axis, s, msg, ref):
        i = (axis * 2 + (0 if s == PLUS else 1)) * PER_LINK + msg
        return pltpu.make_async_remote_copy(
            src_ref=ref, dst_ref=ref, send_sem=g_send.at[g, i], recv_sem=g_recv.at[g, i],
            device_id=(f, wide_of(vec(axis, s))), device_id_type=MESH,
        )

    def gsend(g, axis, s, msg, ref):
        copy = gcopy(g, axis, s, msg, ref)
        copy.start()
        sends.append(copy)

    def gwait(g, axis, s, msg, ref):
        gcopy(g, axis, s, msg, ref).wait_recv()

    def quart(s):
        return 0 if s == PLUS else 1

    here = (0, 0)

    def g_own(g):
        for axis, s in DIRS:
            gsend(g, axis, s, D1, region(g, here, axis))
        for axis, s in DIRS:
            gsend(g, axis, s, OWN, region(g, here, 1 - axis))

    def g_d1(g):
        for axis, s in DIRS:
            off = vec(axis, -s)
            gwait(g, axis, s, D1, region(g, off, axis))
            gsend(g, axis, s, R1, region(g, off, axis, quart(s)))
            for t in (PLUS, MINUS):
                gsend(g, 1 - axis, t, NEAR_M if s == PLUS else NEAR_P, region(g, off, axis))

    def g_r1(g):
        for axis, s in DIRS:
            ref = region(g, vec(axis, 2), axis, quart(s))
            gwait(g, axis, s, R1, ref)
            for t in (PLUS, MINUS):
                gsend(g, 1 - axis, t, OPP_A if s == PLUS else OPP_B, ref)

    def g_d2own(g):
        for axis, s in DIRS:
            off = vec(axis, -s)
            gwait(g, axis, s, OWN, region(g, off, 1 - axis))
            gsend(g, axis, s, R_OWN, region(g, off, 1 - axis, quart(s)))

    def g_d2near(g):
        for j, msg, relay in ((MINUS, NEAR_M, R_NEAR_M), (PLUS, NEAR_P, R_NEAR_P)):
            for axis, s in DIRS:
                off = add(vec(axis, -s), vec(1 - axis, j))
                gwait(g, axis, s, msg, region(g, off, 1 - axis))
                gsend(g, axis, s, relay, region(g, off, 1 - axis, quart(s)))

    def g_d2opp(g):
        for axis, s in DIRS:
            off = add(vec(axis, -s), vec(1 - axis, 2))
            for q, msg in ((0, OPP_A), (1, OPP_B)):
                ref = region(g, off, 1 - axis, q)
                gwait(g, axis, s, msg, ref)
                if q == quart(s):
                    gsend(g, axis, s, R_OPP, ref)

    def g_r2(g, msg, j):
        for axis, s in DIRS:
            off = add(vec(axis, 2), vec(1 - axis, j))
            gwait(g, axis, s, msg, region(g, off, 1 - axis, quart(s)))

    def g_r2all(g):
        for msg, j in ((R_OWN, 0), (R_NEAR_M, MINUS), (R_NEAR_P, PLUS), (R_OPP, 2)):
            g_r2(g, msg, j)

    barrier = pltpu.get_barrier_semaphore()
    for axis, s in DIRS:
        pl.semaphore_signal(barrier, inc=1, device_id=(f, wide_of(vec(axis, s))), device_id_type=MESH)
    for d in range(1, 8):
        pl.semaphore_signal(barrier, inc=1, device_id=((f + d) % 8, w), device_id_type=MESH)

    own = pl.ds(pl.multiple_of(w * pb, pb), pb)
    loads = []
    for c in range(chunks):
        cols = pl.ds(c * CHUNK, CHUNK)
        loads.append(pltpu.make_async_copy(rhs_hbm.at[:, cols], rbuf.at[c, own], loc.at[c]))
    smalls = [
        pltpu.make_async_copy(rows_hbm, rows_ref, loc.at[chunks + 3]),
        pltpu.make_async_copy(owner_hbm, owner_ref, loc.at[chunks + 4]),
        pltpu.make_async_copy(count_hbm, count_ref, loc.at[chunks + 5]),
    ]
    loads.append(pltpu.make_async_copy(inv_hbm, inv, loc.at[chunks]))
    loads.append(pltpu.make_async_copy(below_hbm, below, loc.at[chunks + 1]))
    loads.append(pltpu.make_async_copy(parent_hbm, parent, loc.at[chunks + 2]))
    for copy in loads[:chunks] + smalls + loads[chunks:]:
        copy.start()

    pl.semaphore_wait(barrier, 11)

    loads[0].wait()
    g_own(0)
    loads[1].wait()

    def alive(j):
        return w * tiles + j < count_ref[f]

    def slots_of_tiles():
        for copy in smalls:
            copy.wait()
        none = jnp.full((1, height), parent_rows, jnp.int32)
        rows_out[...] = jnp.full(rows_out.shape, parent_rows, jnp.int32)
        for g in range(8):
            index = [jnp.int32(0)] * slots
            found = [jnp.int32(0)] * slots
            seen = jnp.int32(0)
            for j in range(tiles):
                hit = owner_ref[j] == g
                for k in range(slots):
                    this = jnp.logical_and(hit, seen == k)
                    index[k] = jnp.where(this, j, index[k])
                    found[k] = jnp.where(jnp.logical_and(this, alive(j)), 1, found[k])
                seen = seen + jnp.where(hit, 1, 0)
            for k in range(slots):
                slot_idx[g * slots + k] = index[k]
                rows_out[g, k:k + 1, :] = jnp.where(found[k] == 1, rows_ref[index[k]], none)
        rows_in[f] = rows_out[f]
        for d in range(1, 8):
            to = (f + d) % 8
            copy = pltpu.make_async_remote_copy(
                src_ref=rows_out.at[to], dst_ref=rows_in.at[f], send_sem=r_send.at[d], recv_sem=r_recv.at[d],
                device_id=(to, w), device_id_type=MESH,
            )
            copy.start()
            sends.append(copy)

    def wait_rows():
        for d in range(1, 8):
            pltpu.make_async_remote_copy(
                src_ref=rows_in.at[(f + 8 - d) % 8], dst_ref=rows_in.at[(f + 8 - d) % 8],
                send_sem=r_send.at[d], recv_sem=r_recv.at[d], device_id=((f + d) % 8, w), device_id_type=MESH,
            ).wait_recv()

    def build_hits():
        position = lax.broadcasted_iota(jnp.int32, (parent_rows, height), 0)

        def one(i, carry):
            for k in range(slots):
                row = rows_in[i, k:k + 1, :]
                at = pl.ds(pl.multiple_of((i * slots + k) * height, height), height)
                hits[:, at] = jnp.where(position == row, 1.0, 0.0).astype(jnp.bfloat16)
            return carry

        lax.fori_loop(0, 8, one, 0)

    def block(ref, acc, src, k):
        at = pl.ds(pl.multiple_of(k * pb, pb), pb)
        acc[...] += jnp.dot(ref[:, at], src[at, :], preferred_element_type=jnp.float32)

    def mm(ref, acc, src, lo, hi, place=lambda i: i):
        def step(i, carry):
            block(ref, acc, src, place(i))
            return carry

        lax.fori_loop(lo, hi, step, 0)

    def xcopy(c, sid, rid, src, dst, to):
        return pltpu.make_async_remote_copy(
            src_ref=src, dst_ref=dst, send_sem=x_send.at[c, sid], recv_sem=x_recv.at[c, rid],
            device_id=(to, w), device_id_type=MESH,
        )

    def xstart(*args):
        copy = xcopy(*args)
        copy.start()
        sends.append(copy)

    def chip_at(k):
        return (chip + k + 4) % 4

    def pack(c):
        for j in range(tiles):
            value = u_acc[j * height:(j + 1) * height, :]
            u_tiles[j] = jnp.where(alive(j), value, jnp.zeros_like(value)).astype(jnp.bfloat16)

        def one(i, carry):
            for k in range(slots):
                packed[c, i, k] = u_tiles[slot_idx[i * slots + k]]
            return carry

        lax.fori_loop(0, 8, one, 0)
        for k in range(slots):
            arrived[c, f, k] = packed[c, f, k]

    def xsend(c):
        for n, s in enumerate((PLUS, MINUS)):
            for c2 in range(2):
                to = chip_at(2) * 2 + c2
                xstart(c, 5 + n * 2 + c2, 5 + n * 2 + c2, packed.at[c, to, n], relayed.at[c, n, c2], chip_at(s) * 2 + core)
        for n, s in enumerate((PLUS, MINUS)):
            for c2 in range(2):
                to = chip_at(s) * 2 + c2
                xstart(c, 1 + n * 2 + c2, 1 + n * 2 + core, packed.at[c, to], arrived.at[c, f], to)
        to = chip * 2 + 1 - core
        xstart(c, 0, 0, packed.at[c, to], arrived.at[c, f], to)

    def xrelay(c):
        for n, s in enumerate((PLUS, MINUS)):
            for c2 in range(2):
                ref = relayed.at[c, n, c2]
                xcopy(c, 5 + n * 2 + c2, 5 + n * 2 + c2, ref, ref, chip_at(s) * 2 + core).wait_recv()
                source = chip_at(-s) * 2 + core
                xstart(c, 9 + n * 2 + c2, 9 + n * 2 + core, ref, arrived.at[c, source, n], chip_at(s) * 2 + c2)

    def xwait(c):
        other = chip * 2 + 1 - core
        ref = arrived.at[c, other]
        xcopy(c, 0, 0, ref, ref, other).wait_recv()
        for n, s in enumerate((PLUS, MINUS)):
            for c2 in range(2):
                ref = arrived.at[c, chip_at(-s) * 2 + c2]
                xcopy(c, 0, 1 + n * 2 + c2, ref, ref, other).wait_recv()
        for n, s in enumerate((PLUS, MINUS)):
            for c2 in range(2):
                ref = arrived.at[c, chip_at(2) * 2 + c2, n]
                xcopy(c, 0, 9 + n * 2 + c2, ref, ref, other).wait_recv()

    def scatter(c):
        cols = slice(c * CHUNK, (c + 1) * CHUNK)
        per = 4 * slots * height

        def step(i, acc):
            at = pl.ds(pl.multiple_of(i * per, per), per)
            values = arrived[c, pl.ds(i * 4, 4)].reshape(per, CHUNK)
            return acc - jnp.dot(hits[:, at], values, preferred_element_type=jnp.float32)

        parent_out[:, cols] = step(1, step(0, parent[:, cols].astype(jnp.float32)))

    def sign(i):
        return 2 * (i % 2) - 1

    def at_near(i):
        return wide_of((sign(i) * (1 - i // 2), sign(i) * (i // 2)))

    def at_diagonal(i):
        return wide_of((sign(i), 2 * (i // 2) - 1))

    def at_far(i):
        return wide_of((2 * i, 2 - 2 * i))

    def at_farther(i, j):
        return wide_of((2 * (1 - i) + j * i, j * (1 - i) + 2 * i))

    sides = [(inv, s_acc)] * chunks + [(below, u_acc)] * chunks

    def take(g, count, place):
        mm(sides[g][0], sides[g][1], bufs[g], 0, count, place)

    def take_own(g):
        acc = sides[g][1]
        acc[...] = jnp.zeros_like(acc)
        take(g, 1, lambda i: w)

    def late_first(g):
        g_r2(g, R_OWN, 0)
        take(g, 2, at_far)

    def late_last(g):
        g_r2(g, R_NEAR_M, MINUS)
        take(g, 2, lambda i: at_farther(i, MINUS))
        g_r2(g, R_NEAR_P, PLUS)
        take(g, 2, lambda i: at_farther(i, PLUS))
        g_r2(g, R_OPP, 2)
        take(g, 1, lambda i: wide_of((2, 2)))

    def store_solved(c):
        value = s_acc[...].astype(jnp.bfloat16)
        sbuf[c, own, :] = value
        solved_out[:, c * CHUNK:(c + 1) * CHUNK] = value

    g_own(1)
    slots_of_tiles()
    g_d1(0)
    g_r1(0)
    loads[2].wait()
    take_own(0)
    g_d2own(0)
    take(0, 4, at_near)
    g_d2near(0)
    g_d1(1)
    take(0, 4, at_diagonal)
    g_d2opp(0)
    wait_rows()
    build_hits()
    g_r1(1)
    late_first(0)
    g_d2own(1)
    late_last(0)
    store_solved(0)
    g_own(2)
    take_own(1)
    take(1, 4, at_near)
    g_d2near(1)
    g_d1(2)
    take(1, 4, at_diagonal)
    g_d2opp(1)
    g_r1(2)
    late_first(1)
    g_d2own(2)
    late_last(1)
    store_solved(1)
    g_own(3)
    loads[3].wait()
    take_own(2)
    take(2, 4, at_near)
    g_d2near(2)
    g_d1(3)
    take(2, 4, at_diagonal)
    g_d2opp(2)
    g_r1(3)
    late_first(2)
    g_d2own(3)
    late_last(2)
    pack(0)
    xsend(0)
    take_own(3)
    take(3, 4, at_near)
    g_d2near(3)
    xrelay(0)
    take(3, 4, at_diagonal)
    g_d2opp(3)
    late_first(3)
    late_last(3)
    pack(1)
    xsend(1)
    loads[4].wait()
    xwait(0)
    scatter(0)
    xrelay(1)
    xwait(1)
    scatter(1)
    for copy in sends:
        copy.wait_send()


def write_kernel(solved_in, parent_in, solved_hbm, parent_hbm, sem):
    copies = [
        pltpu.make_async_copy(solved_in, solved_hbm, sem.at[0]),
        pltpu.make_async_copy(parent_in, parent_hbm, sem.at[1]),
    ]
    for copy in copies:
        copy.start()
    for copy in copies:
        copy.wait()


def call(inv, below, rhs, parent_rhs, tile_rows, owners, tile_count):
    rows, pivots = inv.shape
    under = below.shape[0]
    width = rhs.shape[1]
    chunks = width // CHUNK
    tiles, _, height = tile_rows.shape
    slots = 2
    parent_rows = parent_rhs.shape[0]
    bf, f32 = jnp.bfloat16, jnp.float32
    anyspace = pl.BlockSpec(memory_space=pl.ANY)
    hbm = pl.BlockSpec(memory_space=pltpu.HBM)
    vmem = pl.BlockSpec(memory_space=pltpu.VMEM)
    dma = pltpu.SemaphoreType.DMA
    solved, parent_new = pl.pallas_call(
        kernel,
        out_shape=(
            pltpu.VMEM((rows, width), bf),
            pltpu.VMEM((parent_rows, width), f32),
        ),
        in_specs=[hbm] * 7,
        out_specs=(vmem, vmem),
        scratch_shapes=[
            pltpu.VMEM((rows, pivots), bf),
            pltpu.VMEM((under, pivots), bf),
            pltpu.VMEM((chunks, pivots, CHUNK), bf),
            pltpu.VMEM((chunks, pivots, CHUNK), bf),
            pltpu.VMEM((rows, CHUNK), f32),
            pltpu.VMEM((under, CHUNK), f32),
            pltpu.VMEM((tiles, height, CHUNK), bf),
            pltpu.SMEM((8 * slots,), jnp.int32),
            pltpu.VMEM((8, 8, height), jnp.int32),
            pltpu.VMEM((8, 8, height), jnp.int32),
            pltpu.VMEM((chunks, 8, slots, height, CHUNK), bf),
            pltpu.VMEM((chunks, 8, slots, height, CHUNK), bf),
            pltpu.VMEM((chunks, 2, 2, height, CHUNK), bf),
            pltpu.VMEM((parent_rows, 8 * slots * height), bf),
            pltpu.VMEM((parent_rows, width), bf),
            pltpu.VMEM(tile_rows.shape, jnp.int32),
            pltpu.SMEM(owners.shape, jnp.int32),
            pltpu.SMEM(tile_count.shape, jnp.int32),
            dma((2 * chunks, 4 * PER_LINK)),
            dma((2 * chunks, 4 * PER_LINK)),
            dma((chunks, 13)),
            dma((chunks, 13)),
            dma((8,)),
            dma((8,)),
            dma((chunks + 6,)),
        ],
        compiler_params=pltpu.CompilerParams(
            collective_id=0, has_side_effects=True, vmem_limit_bytes=60 * 1024 * 1024
        ),
        name="solve_extend_add",
    )(inv, below, rhs, parent_rhs, tile_rows, owners, tile_count)
    return pl.pallas_call(
        write_kernel,
        out_shape=(
            jax.ShapeDtypeStruct((rows, width), bf),
            jax.ShapeDtypeStruct((parent_rows, width), f32),
        ),
        in_specs=[anyspace] * 2,
        out_specs=(anyspace, anyspace),
        scratch_shapes=[dma((2,))],
        compiler_params=pltpu.CompilerParams(vmem_limit_bytes=1024 * 1024),
        name="write",
    )(solved, parent_new)


def body(inv_diag, below, rhs, tile_count, tile_owner, tile_rows, parent_rhs):
    solved, parent_new = call(
        inv_diag[0], below[0], rhs[0], parent_rhs[0], tile_rows.transpose(1, 0, 2), tile_owner[0, :, 0], tile_count
    )
    return solved[None], parent_new[None]


def solution(mesh):
    spec = P("front", "wide", None)
    return jax.shard_map(
        body,
        mesh=mesh,
        in_specs=(spec, spec, spec, P(), spec, spec, spec),
        out_specs=(spec, spec),
        check_vma=False,
    )
```

```python
import functools

import jax
import jax.numpy as jnp
from jax import lax
from jax.experimental import pallas as pl
from jax.experimental.pallas import tpu as pltpu
from jax.sharding import PartitionSpec as P

MESH = pl.DeviceIdType.MESH
CHUNK = 128
PLUS, MINUS = 1, -1
DIRS = [(a, s) for a in (0, 1) for s in (PLUS, MINUS)]
D1, R1, OWN, NEAR_M, NEAR_P, OPP_A, OPP_B, R_OWN, R_NEAR_M, R_NEAR_P, R_OPP = range(11)
PER_LINK = 11


def kernel(
    inv_hbm, below_hbm, rhs_hbm, parent_hbm, rows_hbm, owner_hbm, count_hbm,
    solved_out, parent_out,
    inv, below, rbuf, sbuf, s_acc, u_acc, u_tiles, slot_idx,
    rows_out, rows_in, packed, arrived, hits, parent, rows_ref, owner_ref, count_ref,
    g_send, g_recv, x_send, x_recv, r_send, r_recv, loc,
):
    f = lax.axis_index("front")
    w = lax.axis_index("wide")
    z, y = w // 4, w % 4
    chip, core = f // 2, f % 2
    pb = rbuf.shape[1] // 16
    half, quarter = pb // 2, pb // 4
    tiles, height = u_tiles.shape[0], u_tiles.shape[1]
    slots = arrived.shape[2]
    parent_rows = parent.shape[0]
    chunks = rbuf.shape[0]
    bufs = [rbuf.at[c] for c in range(chunks)] + [sbuf.at[c] for c in range(chunks)]
    sends = []

    def wide_of(off):
        return ((z + off[1] + 4) % 4) * 4 + (y + off[0] + 4) % 4

    def vec(axis, k):
        return (k, 0) if axis == 0 else (0, k)

    def add(p, q):
        return (p[0] + q[0], p[1] + q[1])

    def region(g, off, h, q=None):
        start = wide_of(off) * pb + h * half + (0 if q is None else q * quarter)
        size = half if q is None else quarter
        return bufs[g].at[pl.ds(pl.multiple_of(start, quarter), size)]

    def gcopy(g, axis, s, msg, ref):
        i = (axis * 2 + (0 if s == PLUS else 1)) * PER_LINK + msg
        return pltpu.make_async_remote_copy(
            src_ref=ref, dst_ref=ref, send_sem=g_send.at[g, i], recv_sem=g_recv.at[g, i],
            device_id=(f, wide_of(vec(axis, s))), device_id_type=MESH,
        )

    def gsend(g, axis, s, msg, ref):
        copy = gcopy(g, axis, s, msg, ref)
        copy.start()
        sends.append(copy)

    def gwait(g, axis, s, msg, ref):
        gcopy(g, axis, s, msg, ref).wait_recv()

    def quart(s):
        return 0 if s == PLUS else 1

    here = (0, 0)

    def g_own(g):
        for axis, s in DIRS:
            gsend(g, axis, s, D1, region(g, here, axis))
        for axis, s in DIRS:
            gsend(g, axis, s, OWN, region(g, here, 1 - axis))

    def g_d1(g):
        def near(axis, s):
            for t in (PLUS, MINUS):
                gsend(g, 1 - axis, t, NEAR_M if s == PLUS else NEAR_P, region(g, vec(axis, -s), axis))

        for axis, s in DIRS:
            off = vec(axis, -s)
            gwait(g, axis, s, D1, region(g, off, axis))
            gsend(g, axis, s, R1, region(g, off, axis, quart(s)))
        for axis, s in DIRS:
            near(axis, s)

    def g_r1(g):
        for axis, s in DIRS:
            ref = region(g, vec(axis, 2), axis, quart(s))
            gwait(g, axis, s, R1, ref)
            for t in (PLUS, MINUS):
                gsend(g, 1 - axis, t, OPP_A if s == PLUS else OPP_B, ref)

    def g_d2own(g):
        for axis, s in DIRS:
            off = vec(axis, -s)
            gwait(g, axis, s, OWN, region(g, off, 1 - axis))
            gsend(g, axis, s, R_OWN, region(g, off, 1 - axis, quart(s)))

    def g_d2near(g):
        for j, msg, relay in ((MINUS, NEAR_M, R_NEAR_M), (PLUS, NEAR_P, R_NEAR_P)):
            for axis, s in DIRS:
                off = add(vec(axis, -s), vec(1 - axis, j))
                gwait(g, axis, s, msg, region(g, off, 1 - axis))
                gsend(g, axis, s, relay, region(g, off, 1 - axis, quart(s)))

    def g_d2opp(g):
        for axis, s in DIRS:
            off = add(vec(axis, -s), vec(1 - axis, 2))
            for q, msg in ((0, OPP_A), (1, OPP_B)):
                ref = region(g, off, 1 - axis, q)
                gwait(g, axis, s, msg, ref)
                if q == quart(s):
                    gsend(g, axis, s, R_OPP, ref)

    def g_r2(g, msg, j):
        for axis, s in DIRS:
            off = add(vec(axis, 2), vec(1 - axis, j))
            gwait(g, axis, s, msg, region(g, off, 1 - axis, quart(s)))

    def g_r2all(g):
        for msg, j in ((R_OWN, 0), (R_NEAR_M, MINUS), (R_NEAR_P, PLUS), (R_OPP, 2)):
            g_r2(g, msg, j)

    barrier = pltpu.get_barrier_semaphore()
    for axis, s in DIRS:
        pl.semaphore_signal(barrier, inc=1, device_id=(f, wide_of(vec(axis, s))), device_id_type=MESH)
    for d in range(1, 8):
        pl.semaphore_signal(barrier, inc=1, device_id=((f + d) % 8, w), device_id_type=MESH)

    own = pl.ds(pl.multiple_of(w * pb, pb), pb)
    loads = []
    for c in range(chunks):
        cols = pl.ds(c * CHUNK, CHUNK)
        loads.append(pltpu.make_async_copy(rhs_hbm.at[:, cols], rbuf.at[c, own], loc.at[c]))
    smalls = [
        pltpu.make_async_copy(rows_hbm, rows_ref, loc.at[chunks + 3]),
        pltpu.make_async_copy(owner_hbm, owner_ref, loc.at[chunks + 4]),
        pltpu.make_async_copy(count_hbm, count_ref, loc.at[chunks + 5]),
    ]
    loads.append(pltpu.make_async_copy(inv_hbm, inv, loc.at[chunks]))
    loads.append(pltpu.make_async_copy(below_hbm, below, loc.at[chunks + 1]))
    loads.append(pltpu.make_async_copy(parent_hbm, parent, loc.at[chunks + 2]))
    for copy in loads[:chunks] + smalls + loads[chunks:]:
        copy.start()

    pl.semaphore_wait(barrier, 11)

    loads[0].wait()
    g_own(0)
    loads[1].wait()
    g_own(1)

    def alive(j):
        return w * tiles + j < count_ref[f]

    def slots_of_tiles():
        for copy in smalls:
            copy.wait()
        none = jnp.full((1, height), parent_rows, jnp.int32)
        rows_out[...] = jnp.full(rows_out.shape, parent_rows, jnp.int32)
        for g in range(8):
            index = [jnp.int32(0)] * slots
            found = [jnp.int32(0)] * slots
            seen = jnp.int32(0)
            for j in range(tiles):
                hit = owner_ref[j] == g
                for k in range(slots):
                    this = jnp.logical_and(hit, seen == k)
                    index[k] = jnp.where(this, j, index[k])
                    found[k] = jnp.where(jnp.logical_and(this, alive(j)), 1, found[k])
                seen = seen + jnp.where(hit, 1, 0)
            for k in range(slots):
                slot_idx[g * slots + k] = index[k]
                rows_out[g, k:k + 1, :] = jnp.where(found[k] == 1, rows_ref[index[k]], none)
        rows_in[f] = rows_out[f]
        for d in range(1, 8):
            to = (f + d) % 8
            copy = pltpu.make_async_remote_copy(
                src_ref=rows_out.at[to], dst_ref=rows_in.at[f], send_sem=r_send.at[d], recv_sem=r_recv.at[d],
                device_id=(to, w), device_id_type=MESH,
            )
            copy.start()
            sends.append(copy)

    def wait_rows():
        for d in range(1, 8):
            pltpu.make_async_remote_copy(
                src_ref=rows_in.at[(f + 8 - d) % 8], dst_ref=rows_in.at[(f + 8 - d) % 8],
                send_sem=r_send.at[d], recv_sem=r_recv.at[d], device_id=((f + d) % 8, w), device_id_type=MESH,
            ).wait_recv()

    def build_hits():
        position = lax.broadcasted_iota(jnp.int32, (parent_rows, height), 0)

        def one(i, carry):
            for k in range(slots):
                row = rows_in[i, k:k + 1, :]
                at = pl.ds(pl.multiple_of((i * slots + k) * height, height), height)
                hits[:, at] = jnp.where(position == row, 1.0, 0.0).astype(jnp.bfloat16)
            return carry

        lax.fori_loop(0, 8, one, 0)

    def block(ref, acc, src, k):
        at = pl.ds(pl.multiple_of(k * pb, pb), pb)
        acc[...] += jnp.dot(ref[:, at], src[at, :], preferred_element_type=jnp.float32)

    def mm(ref, acc, src, lo, hi, place=lambda i: i):
        def step(i, carry):
            block(ref, acc, src, place(i))
            return carry

        lax.fori_loop(lo, hi, step, 0)

    def xcopy(c, sid, rid, src, dst, to):
        return pltpu.make_async_remote_copy(
            src_ref=src, dst_ref=dst, send_sem=x_send.at[c, sid], recv_sem=x_recv.at[c, rid],
            device_id=(to, w), device_id_type=MESH,
        )

    def xstart(*args):
        copy = xcopy(*args)
        copy.start()
        sends.append(copy)

    def chip_at(k):
        return (chip + k + 4) % 4

    def pack(c):
        for j in range(tiles):
            value = u_acc[j * height:(j + 1) * height, :]
            u_tiles[j] = jnp.where(alive(j), value, jnp.zeros_like(value)).astype(jnp.bfloat16)

    def pack_for(c, to):
        for k in range(slots):
            packed[c, to, k] = u_tiles[slot_idx[to * slots + k]]

    def xsend(c):
        for c2 in range(2):
            to = chip_at(2) * 2 + c2
            pack_for(c, to)
            xstart(c, 5 + c2, 5 + core, packed.at[c, to], arrived.at[c, f], to)
        for n, s in enumerate((PLUS, MINUS)):
            for c2 in range(2):
                to = chip_at(s) * 2 + c2
                pack_for(c, to)
                xstart(c, 1 + n * 2 + c2, 1 + n * 2 + core, packed.at[c, to], arrived.at[c, f], to)
        to = chip * 2 + 1 - core
        pack_for(c, to)
        xstart(c, 0, 0, packed.at[c, to], arrived.at[c, f], to)
        for k in range(slots):
            arrived[c, f, k] = u_tiles[slot_idx[f * slots + k]]

    def add_chip(c, k):
        other = chip * 2 + 1 - core
        if k == 0:
            ref = arrived.at[c, other]
            xcopy(c, 0, 0, ref, ref, other).wait_recv()
        else:
            first = {-1: 1, 1: 3, 2: 5}[k]
            for c2 in range(2):
                ref = arrived.at[c, chip_at(k) * 2 + c2]
                xcopy(c, 0, first + c2, ref, ref, other).wait_recv()
        cols = slice(c * CHUNK, (c + 1) * CHUNK)
        per = 2 * slots * height
        values = arrived[c, pl.ds(chip_at(k) * 2, 2)].reshape(per, CHUNK)
        at = pl.ds(pl.multiple_of(chip_at(k) * per, per), per)
        before = parent[:, cols].astype(jnp.float32) if k == 0 else parent_out[:, cols]
        parent_out[:, cols] = before - jnp.dot(hits[:, at], values, preferred_element_type=jnp.float32)

    def sign(i):
        return 2 * (i % 2) - 1

    def at_near(i):
        return wide_of((sign(i) * (1 - i // 2), sign(i) * (i // 2)))

    def at_diagonal(i):
        return wide_of((sign(i), 2 * (i // 2) - 1))

    def at_far(i):
        return wide_of((2 * i, 2 - 2 * i))

    def at_farther(i, j):
        return wide_of((2 * (1 - i) + j * i, j * (1 - i) + 2 * i))

    sides = [(inv, s_acc)] * chunks + [(below, u_acc)] * chunks

    def take(g, count, place):
        mm(sides[g][0], sides[g][1], bufs[g], 0, count, place)

    def take_own(g):
        acc = sides[g][1]
        acc[...] = jnp.zeros_like(acc)
        take(g, 1, lambda i: w)

    def late_first(g):
        g_r2(g, R_OWN, 0)
        take(g, 2, at_far)

    def late_last(g):
        g_r2(g, R_NEAR_M, MINUS)
        take(g, 2, lambda i: at_farther(i, MINUS))
        g_r2(g, R_NEAR_P, PLUS)
        take(g, 2, lambda i: at_farther(i, PLUS))
        g_r2(g, R_OPP, 2)
        take(g, 1, lambda i: wide_of((2, 2)))

    def store_solved(c):
        value = s_acc[...].astype(jnp.bfloat16)
        sbuf[c, own, :] = value
        solved_out[:, c * CHUNK:(c + 1) * CHUNK] = value

    slots_of_tiles()
    g_d1(0)
    g_r1(0)
    loads[2].wait()
    take_own(0)
    g_d2own(0)
    take(0, 4, at_near)
    g_d2near(0)
    g_d1(1)
    take(0, 4, at_diagonal)
    g_d2opp(0)
    wait_rows()
    build_hits()
    g_r1(1)
    late_first(0)
    g_d2own(1)
    late_last(0)
    store_solved(0)
    g_own(2)
    take_own(1)
    take(1, 4, at_near)
    g_d2near(1)
    g_d1(2)
    take(1, 4, at_diagonal)
    g_d2opp(1)
    g_r1(2)
    late_first(1)
    g_d2own(2)
    late_last(1)
    store_solved(1)
    g_own(3)
    loads[3].wait()
    take_own(2)
    take(2, 4, at_near)
    g_d2near(2)
    g_d1(3)
    take(2, 4, at_diagonal)
    g_d2opp(2)
    g_r1(3)
    late_first(2)
    g_d2own(3)
    late_last(2)
    pack(0)
    xsend(0)
    take_own(3)
    take(3, 4, at_near)
    g_d2near(3)
    take(3, 4, at_diagonal)
    g_d2opp(3)
    late_first(3)
    late_last(3)
    pack(1)
    xsend(1)
    loads[4].wait()
    for k in (0, -1, 1, 2):
        add_chip(0, k)
    for k in (0, -1, 1, 2):
        add_chip(1, k)
    for copy in sends:
        copy.wait_send()


def write_kernel(solved_in, parent_in, solved_hbm, parent_hbm, sem):
    copies = [
        pltpu.make_async_copy(solved_in, solved_hbm, sem.at[0]),
        pltpu.make_async_copy(parent_in, parent_hbm, sem.at[1]),
    ]
    for copy in copies:
        copy.start()
    for copy in copies:
        copy.wait()


def call(inv, below, rhs, parent_rhs, tile_rows, owners, tile_count):
    rows, pivots = inv.shape
    under = below.shape[0]
    width = rhs.shape[1]
    chunks = width // CHUNK
    tiles, _, height = tile_rows.shape
    slots = 2
    parent_rows = parent_rhs.shape[0]
    bf, f32 = jnp.bfloat16, jnp.float32
    anyspace = pl.BlockSpec(memory_space=pl.ANY)
    hbm = pl.BlockSpec(memory_space=pltpu.HBM)
    vmem = pl.BlockSpec(memory_space=pltpu.VMEM)
    dma = pltpu.SemaphoreType.DMA
    solved, parent_new = pl.pallas_call(
        kernel,
        out_shape=(
            pltpu.VMEM((rows, width), bf),
            pltpu.VMEM((parent_rows, width), f32),
        ),
        in_specs=[hbm] * 7,
        out_specs=(vmem, vmem),
        scratch_shapes=[
            pltpu.VMEM((rows, pivots), bf),
            pltpu.VMEM((under, pivots), bf),
            pltpu.VMEM((chunks, pivots, CHUNK), bf),
            pltpu.VMEM((chunks, pivots, CHUNK), bf),
            pltpu.VMEM((rows, CHUNK), f32),
            pltpu.VMEM((under, CHUNK), f32),
            pltpu.VMEM((tiles, height, CHUNK), bf),
            pltpu.SMEM((8 * slots,), jnp.int32),
            pltpu.VMEM((8, 8, height), jnp.int32),
            pltpu.VMEM((8, 8, height), jnp.int32),
            pltpu.VMEM((chunks, 8, slots, height, CHUNK), bf),
            pltpu.VMEM((chunks, 8, slots, height, CHUNK), bf),
            pltpu.VMEM((parent_rows, 8 * slots * height), bf),
            pltpu.VMEM((parent_rows, width), bf),
            pltpu.VMEM(tile_rows.shape, jnp.int32),
            pltpu.SMEM(owners.shape, jnp.int32),
            pltpu.SMEM(tile_count.shape, jnp.int32),
            dma((2 * chunks, 4 * PER_LINK)),
            dma((2 * chunks, 4 * PER_LINK)),
            dma((chunks, 7)),
            dma((chunks, 7)),
            dma((8,)),
            dma((8,)),
            dma((chunks + 6,)),
        ],
        compiler_params=pltpu.CompilerParams(
            collective_id=0, has_side_effects=True, vmem_limit_bytes=60 * 1024 * 1024
        ),
        name="solve_extend_add",
    )(inv, below, rhs, parent_rhs, tile_rows, owners, tile_count)
    return pl.pallas_call(
        write_kernel,
        out_shape=(
            jax.ShapeDtypeStruct((rows, width), bf),
            jax.ShapeDtypeStruct((parent_rows, width), f32),
        ),
        in_specs=[anyspace] * 2,
        out_specs=(anyspace, anyspace),
        scratch_shapes=[dma((2,))],
        compiler_params=pltpu.CompilerParams(vmem_limit_bytes=1024 * 1024),
        name="write",
    )(solved, parent_new)


def body(inv_diag, below, rhs, tile_count, tile_owner, tile_rows, parent_rhs):
    solved, parent_new = call(
        inv_diag[0], below[0], rhs[0], parent_rhs[0], tile_rows.transpose(1, 0, 2), tile_owner[0, :, 0], tile_count
    )
    return solved[None], parent_new[None]


def solution(mesh):
    spec = P("front", "wide", None)
    return jax.shard_map(
        body,
        mesh=mesh,
        in_specs=(spec, spec, spec, P(), spec, spec, spec),
        out_specs=(spec, spec),
        check_vma=False,
    )
```

```python
import functools

import jax
import jax.numpy as jnp
from jax import lax
from jax.experimental import pallas as pl
from jax.experimental.pallas import tpu as pltpu
from jax.sharding import PartitionSpec as P

MESH = pl.DeviceIdType.MESH
CHUNK = 128
PLUS, MINUS = 1, -1
DIRS = [(a, s) for a in (0, 1) for s in (PLUS, MINUS)]
D1, R1, OWN, NEAR_M, NEAR_P, OPP_A, OPP_B, R_OWN, R_NEAR_M, R_NEAR_P, R_OPP = range(11)
PER_LINK = 11


def kernel(
    inv_hbm, below_hbm, rhs_hbm, parent_hbm, rows_hbm, owner_hbm, count_hbm,
    solved_out, parent_out,
    inv, below, rbuf, sbuf, s_acc, u_acc, u_tiles, slot_idx,
    rows_out, rows_in, packed, arrived, hits, parent, rows_ref, owner_ref, count_ref,
    g_send, g_recv, x_send, x_recv, r_send, r_recv, loc,
):
    f = lax.axis_index("front")
    w = lax.axis_index("wide")
    z, y = w // 4, w % 4
    chip, core = f // 2, f % 2
    pb = rbuf.shape[1] // 16
    half, quarter = pb // 2, pb // 4
    tiles, height = u_tiles.shape[0], u_tiles.shape[1]
    slots = arrived.shape[2]
    parent_rows = parent.shape[0]
    chunks = rbuf.shape[0]
    bufs = [rbuf.at[c] for c in range(chunks)] + [sbuf.at[c] for c in range(chunks)]
    sends = []

    def wide_of(off):
        return ((z + off[1] + 4) % 4) * 4 + (y + off[0] + 4) % 4

    def vec(axis, k):
        return (k, 0) if axis == 0 else (0, k)

    def add(p, q):
        return (p[0] + q[0], p[1] + q[1])

    def region(g, off, h, q=None):
        start = wide_of(off) * pb + h * half + (0 if q is None else q * quarter)
        size = half if q is None else quarter
        return bufs[g].at[pl.ds(pl.multiple_of(start, quarter), size)]

    def gcopy(g, axis, s, msg, ref):
        i = (axis * 2 + (0 if s == PLUS else 1)) * PER_LINK + msg
        return pltpu.make_async_remote_copy(
            src_ref=ref, dst_ref=ref, send_sem=g_send.at[g, i], recv_sem=g_recv.at[g, i],
            device_id=(f, wide_of(vec(axis, s))), device_id_type=MESH,
        )

    def gsend(g, axis, s, msg, ref):
        copy = gcopy(g, axis, s, msg, ref)
        copy.start()
        sends.append(copy)

    def gwait(g, axis, s, msg, ref):
        gcopy(g, axis, s, msg, ref).wait_recv()

    def quart(s):
        return 0 if s == PLUS else 1

    here = (0, 0)

    def g_own(g):
        for axis, s in DIRS:
            gsend(g, axis, s, D1, region(g, here, axis))
        for axis, s in DIRS:
            gsend(g, axis, s, OWN, region(g, here, 1 - axis))

    def g_d1(g):
        def near(axis, s):
            for t in (PLUS, MINUS):
                gsend(g, 1 - axis, t, NEAR_M if s == PLUS else NEAR_P, region(g, vec(axis, -s), axis))

        for axis, s in DIRS:
            off = vec(axis, -s)
            gwait(g, axis, s, D1, region(g, off, axis))
            gsend(g, axis, s, R1, region(g, off, axis, quart(s)))
        for axis, s in DIRS:
            near(axis, s)

    def g_r1(g):
        for axis, s in DIRS:
            ref = region(g, vec(axis, 2), axis, quart(s))
            gwait(g, axis, s, R1, ref)
            for t in (PLUS, MINUS):
                gsend(g, 1 - axis, t, OPP_A if s == PLUS else OPP_B, ref)

    def g_d2own(g):
        for axis, s in DIRS:
            off = vec(axis, -s)
            gwait(g, axis, s, OWN, region(g, off, 1 - axis))
            gsend(g, axis, s, R_OWN, region(g, off, 1 - axis, quart(s)))

    def g_d2near(g):
        for j, msg, relay in ((MINUS, NEAR_M, R_NEAR_M), (PLUS, NEAR_P, R_NEAR_P)):
            for axis, s in DIRS:
                off = add(vec(axis, -s), vec(1 - axis, j))
                gwait(g, axis, s, msg, region(g, off, 1 - axis))
                gsend(g, axis, s, relay, region(g, off, 1 - axis, quart(s)))

    def g_d2opp(g):
        for axis, s in DIRS:
            off = add(vec(axis, -s), vec(1 - axis, 2))
            for q, msg in ((0, OPP_A), (1, OPP_B)):
                ref = region(g, off, 1 - axis, q)
                gwait(g, axis, s, msg, ref)
                if q == quart(s):
                    gsend(g, axis, s, R_OPP, ref)

    def g_r2(g, msg, j):
        for axis, s in DIRS:
            off = add(vec(axis, 2), vec(1 - axis, j))
            gwait(g, axis, s, msg, region(g, off, 1 - axis, quart(s)))

    def g_r2all(g):
        for msg, j in ((R_OWN, 0), (R_NEAR_M, MINUS), (R_NEAR_P, PLUS), (R_OPP, 2)):
            g_r2(g, msg, j)

    barrier = pltpu.get_barrier_semaphore()
    for axis, s in DIRS:
        pl.semaphore_signal(barrier, inc=1, device_id=(f, wide_of(vec(axis, s))), device_id_type=MESH)
    for d in range(1, 8):
        pl.semaphore_signal(barrier, inc=1, device_id=((f + d) % 8, w), device_id_type=MESH)

    own = pl.ds(pl.multiple_of(w * pb, pb), pb)
    loads = []
    for c in range(chunks):
        cols = pl.ds(c * CHUNK, CHUNK)
        loads.append(pltpu.make_async_copy(rhs_hbm.at[:, cols], rbuf.at[c, own], loc.at[c]))
    smalls = [
        pltpu.make_async_copy(rows_hbm, rows_ref, loc.at[chunks + 3]),
        pltpu.make_async_copy(owner_hbm, owner_ref, loc.at[chunks + 4]),
        pltpu.make_async_copy(count_hbm, count_ref, loc.at[chunks + 5]),
    ]
    loads.append(pltpu.make_async_copy(inv_hbm, inv, loc.at[chunks]))
    loads.append(pltpu.make_async_copy(below_hbm, below, loc.at[chunks + 1]))
    loads.append(pltpu.make_async_copy(parent_hbm, parent, loc.at[chunks + 2]))
    for copy in loads[:chunks] + smalls + loads[chunks:]:
        copy.start()

    pl.semaphore_wait(barrier, 11)

    loads[0].wait()
    g_own(0)
    loads[1].wait()
    g_own(1)

    def alive(j):
        return w * tiles + j < count_ref[f]

    def slots_of_tiles():
        for copy in smalls:
            copy.wait()
        none = jnp.full((1, height), parent_rows, jnp.int32)
        rows_out[...] = jnp.full(rows_out.shape, parent_rows, jnp.int32)
        for g in range(8):
            index = [jnp.int32(0)] * slots
            found = [jnp.int32(0)] * slots
            seen = jnp.int32(0)
            for j in range(tiles):
                hit = owner_ref[j] == g
                for k in range(slots):
                    this = jnp.logical_and(hit, seen == k)
                    index[k] = jnp.where(this, j, index[k])
                    found[k] = jnp.where(jnp.logical_and(this, alive(j)), 1, found[k])
                seen = seen + jnp.where(hit, 1, 0)
            for k in range(slots):
                slot_idx[g * slots + k] = index[k]
                rows_out[g, k:k + 1, :] = jnp.where(found[k] == 1, rows_ref[index[k]], none)
        rows_in[f] = rows_out[f]
        for d in range(1, 8):
            to = (f + d) % 8
            copy = pltpu.make_async_remote_copy(
                src_ref=rows_out.at[to], dst_ref=rows_in.at[f], send_sem=r_send.at[d], recv_sem=r_recv.at[d],
                device_id=(to, w), device_id_type=MESH,
            )
            copy.start()
            sends.append(copy)

    def wait_rows():
        for d in range(1, 8):
            pltpu.make_async_remote_copy(
                src_ref=rows_in.at[(f + 8 - d) % 8], dst_ref=rows_in.at[(f + 8 - d) % 8],
                send_sem=r_send.at[d], recv_sem=r_recv.at[d], device_id=((f + d) % 8, w), device_id_type=MESH,
            ).wait_recv()

    def build_hits():
        position = lax.broadcasted_iota(jnp.int32, (parent_rows, height), 0)

        def one(i, carry):
            for k in range(slots):
                row = rows_in[i, k:k + 1, :]
                at = pl.ds(pl.multiple_of((i * slots + k) * height, height), height)
                hits[:, at] = jnp.where(position == row, 1.0, 0.0).astype(jnp.bfloat16)
            return carry

        lax.fori_loop(0, 8, one, 0)

    def block(ref, acc, src, k):
        at = pl.ds(pl.multiple_of(k * pb, pb), pb)
        acc[...] += jnp.dot(ref[:, at], src[at, :], preferred_element_type=jnp.float32)

    def mm(ref, acc, src, lo, hi, place=lambda i: i):
        def step(i, carry):
            block(ref, acc, src, place(i))
            return carry

        lax.fori_loop(lo, hi, step, 0)

    def xcopy(c, sid, rid, src, dst, to):
        return pltpu.make_async_remote_copy(
            src_ref=src, dst_ref=dst, send_sem=x_send.at[c, sid], recv_sem=x_recv.at[c, rid],
            device_id=(to, w), device_id_type=MESH,
        )

    def xstart(*args):
        copy = xcopy(*args)
        copy.start()
        sends.append(copy)

    def chip_at(k):
        return (chip + k + 4) % 4

    def pack(c):
        for j in range(tiles):
            value = u_acc[j * height:(j + 1) * height, :]
            u_tiles[j] = jnp.where(alive(j), value, jnp.zeros_like(value)).astype(jnp.bfloat16)

    def pack_for(c, to):
        for k in range(slots):
            packed[c, to, k] = u_tiles[slot_idx[to * slots + k]]

    def xsend(c):
        for c2 in range(2):
            to = chip_at(2) * 2 + c2
            pack_for(c, to)
            xstart(c, 5 + c2, 5 + core, packed.at[c, to], arrived.at[c, f], to)
        for n, s in enumerate((PLUS, MINUS)):
            for c2 in range(2):
                to = chip_at(s) * 2 + c2
                pack_for(c, to)
                xstart(c, 1 + n * 2 + c2, 1 + n * 2 + core, packed.at[c, to], arrived.at[c, f], to)
        to = chip * 2 + 1 - core
        pack_for(c, to)
        xstart(c, 0, 0, packed.at[c, to], arrived.at[c, f], to)
        for k in range(slots):
            arrived[c, f, k] = u_tiles[slot_idx[f * slots + k]]

    def add_chip(c, k):
        other = chip * 2 + 1 - core
        if k == 0:
            ref = arrived.at[c, other]
            xcopy(c, 0, 0, ref, ref, other).wait_recv()
        else:
            first = {-1: 1, 1: 3, 2: 5}[k]
            for c2 in range(2):
                ref = arrived.at[c, chip_at(k) * 2 + c2]
                xcopy(c, 0, first + c2, ref, ref, other).wait_recv()
        cols = slice(c * CHUNK, (c + 1) * CHUNK)
        per = 2 * slots * height
        values = arrived[c, pl.ds(chip_at(k) * 2, 2)].reshape(per, CHUNK)
        at = pl.ds(pl.multiple_of(chip_at(k) * per, per), per)
        before = parent[:, cols].astype(jnp.float32) if k == 0 else parent_out[:, cols]
        parent_out[:, cols] = before - jnp.dot(hits[:, at], values, preferred_element_type=jnp.float32)

    def sign(i):
        return 2 * (i % 2) - 1

    def at_near(i):
        return wide_of((sign(i) * (1 - i // 2), sign(i) * (i // 2)))

    def at_diagonal(i):
        return wide_of((sign(i), 2 * (i // 2) - 1))

    def at_far(i):
        return wide_of((2 * i, 2 - 2 * i))

    def at_farther(i, j):
        return wide_of((2 * (1 - i) + j * i, j * (1 - i) + 2 * i))

    sides = [(inv, s_acc)] * chunks + [(below, u_acc)] * chunks

    def take(g, count, place):
        mm(sides[g][0], sides[g][1], bufs[g], 0, count, place)

    def take_own(g):
        acc = sides[g][1]
        acc[...] = jnp.zeros_like(acc)
        take(g, 1, lambda i: w)

    def late_first(g):
        g_r2(g, R_OWN, 0)
        take(g, 2, at_far)

    def late_last(g):
        g_r2(g, R_NEAR_M, MINUS)
        take(g, 2, lambda i: at_farther(i, MINUS))
        g_r2(g, R_NEAR_P, PLUS)
        take(g, 2, lambda i: at_farther(i, PLUS))
        g_r2(g, R_OPP, 2)
        take(g, 1, lambda i: wide_of((2, 2)))

    def store_solved(c):
        value = s_acc[...].astype(jnp.bfloat16)
        sbuf[c, own, :] = value
        solved_out[:, c * CHUNK:(c + 1) * CHUNK] = value

    slots_of_tiles()
    g_d1(0)
    g_r1(0)
    loads[2].wait()
    take_own(0)
    g_d2own(0)
    take(0, 4, at_near)
    g_d2near(0)
    g_d1(1)
    take(0, 4, at_diagonal)
    g_d2opp(0)
    wait_rows()
    build_hits()
    g_r1(1)
    late_first(0)
    g_d2own(1)
    late_last(0)
    store_solved(0)
    g_own(2)
    take_own(1)
    take(1, 4, at_near)
    g_d2near(1)
    g_d1(2)
    take(1, 4, at_diagonal)
    g_d2opp(1)
    g_r1(2)
    late_first(1)
    g_d2own(2)
    late_last(1)
    store_solved(1)
    g_own(3)
    loads[3].wait()
    take_own(2)
    g_d2near(2)
    take(2, 4, at_near)
    g_d2opp(2)
    g_d1(3)
    take(2, 4, at_diagonal)
    late_first(2)
    g_r1(3)
    g_d2own(3)
    late_last(2)
    pack(0)
    xsend(0)
    g_d2near(3)
    take_own(3)
    take(3, 4, at_near)
    g_d2opp(3)
    take(3, 4, at_diagonal)
    late_first(3)
    late_last(3)
    pack(1)
    xsend(1)
    loads[4].wait()
    for k in (0, -1, 1, 2):
        add_chip(0, k)
    for k in (0, -1, 1, 2):
        add_chip(1, k)
    for copy in sends:
        copy.wait_send()


def write_kernel(solved_in, parent_in, solved_hbm, parent_hbm, sem):
    copies = [
        pltpu.make_async_copy(solved_in, solved_hbm, sem.at[0]),
        pltpu.make_async_copy(parent_in, parent_hbm, sem.at[1]),
    ]
    for copy in copies:
        copy.start()
    for copy in copies:
        copy.wait()


def call(inv, below, rhs, parent_rhs, tile_rows, owners, tile_count):
    rows, pivots = inv.shape
    under = below.shape[0]
    width = rhs.shape[1]
    chunks = width // CHUNK
    tiles, _, height = tile_rows.shape
    slots = 2
    parent_rows = parent_rhs.shape[0]
    bf, f32 = jnp.bfloat16, jnp.float32
    anyspace = pl.BlockSpec(memory_space=pl.ANY)
    hbm = pl.BlockSpec(memory_space=pltpu.HBM)
    vmem = pl.BlockSpec(memory_space=pltpu.VMEM)
    dma = pltpu.SemaphoreType.DMA
    solved, parent_new = pl.pallas_call(
        kernel,
        out_shape=(
            pltpu.VMEM((rows, width), bf),
            pltpu.VMEM((parent_rows, width), f32),
        ),
        in_specs=[hbm] * 7,
        out_specs=(vmem, vmem),
        scratch_shapes=[
            pltpu.VMEM((rows, pivots), bf),
            pltpu.VMEM((under, pivots), bf),
            pltpu.VMEM((chunks, pivots, CHUNK), bf),
            pltpu.VMEM((chunks, pivots, CHUNK), bf),
            pltpu.VMEM((rows, CHUNK), f32),
            pltpu.VMEM((under, CHUNK), f32),
            pltpu.VMEM((tiles, height, CHUNK), bf),
            pltpu.SMEM((8 * slots,), jnp.int32),
            pltpu.VMEM((8, 8, height), jnp.int32),
            pltpu.VMEM((8, 8, height), jnp.int32),
            pltpu.VMEM((chunks, 8, slots, height, CHUNK), bf),
            pltpu.VMEM((chunks, 8, slots, height, CHUNK), bf),
            pltpu.VMEM((parent_rows, 8 * slots * height), bf),
            pltpu.VMEM((parent_rows, width), bf),
            pltpu.VMEM(tile_rows.shape, jnp.int32),
            pltpu.SMEM(owners.shape, jnp.int32),
            pltpu.SMEM(tile_count.shape, jnp.int32),
            dma((2 * chunks, 4 * PER_LINK)),
            dma((2 * chunks, 4 * PER_LINK)),
            dma((chunks, 7)),
            dma((chunks, 7)),
            dma((8,)),
            dma((8,)),
            dma((chunks + 6,)),
        ],
        compiler_params=pltpu.CompilerParams(
            collective_id=0, has_side_effects=True, vmem_limit_bytes=60 * 1024 * 1024
        ),
        name="solve_extend_add",
    )(inv, below, rhs, parent_rhs, tile_rows, owners, tile_count)
    return pl.pallas_call(
        write_kernel,
        out_shape=(
            jax.ShapeDtypeStruct((rows, width), bf),
            jax.ShapeDtypeStruct((parent_rows, width), f32),
        ),
        in_specs=[anyspace] * 2,
        out_specs=(anyspace, anyspace),
        scratch_shapes=[dma((2,))],
        compiler_params=pltpu.CompilerParams(vmem_limit_bytes=1024 * 1024),
        name="write",
    )(solved, parent_new)


def body(inv_diag, below, rhs, tile_count, tile_owner, tile_rows, parent_rhs):
    solved, parent_new = call(
        inv_diag[0], below[0], rhs[0], parent_rhs[0], tile_rows.transpose(1, 0, 2), tile_owner[0, :, 0], tile_count
    )
    return solved[None], parent_new[None]


def solution(mesh):
    spec = P("front", "wide", None)
    return jax.shard_map(
        body,
        mesh=mesh,
        in_specs=(spec, spec, spec, P(), spec, spec, spec),
        out_specs=(spec, spec),
        check_vma=False,
    )
```

```python
import functools

import jax
import jax.numpy as jnp
from jax import lax
from jax.experimental import pallas as pl
from jax.experimental.pallas import tpu as pltpu
from jax.sharding import PartitionSpec as P

MESH = pl.DeviceIdType.MESH
CHUNK = 128
PLUS, MINUS = 1, -1
DIRS = [(a, s) for a in (0, 1) for s in (PLUS, MINUS)]
D1, R1, OWN, NEAR_M, NEAR_P, OPP_A, OPP_B, R_OWN, R_NEAR_M, R_NEAR_P, R_OPP = range(11)
PER_LINK = 11


def kernel(
    inv_hbm, below_hbm, rhs_hbm, parent_hbm, rows_hbm, owner_hbm, count_hbm,
    solved_out, parent_out,
    inv, below, rbuf, sbuf, s_acc, u_acc, u_tiles, slot_idx,
    rows_out, rows_in, packed, arrived, hits, parent, rows_ref, owner_ref, count_ref,
    g_send, g_recv, x_send, x_recv, r_send, r_recv, loc,
):
    f = lax.axis_index("front")
    w = lax.axis_index("wide")
    z, y = w // 4, w % 4
    chip, core = f // 2, f % 2
    pb = rbuf.shape[1] // 16
    half, quarter = pb // 2, pb // 4
    tiles, height = u_tiles.shape[0], u_tiles.shape[1]
    slots = arrived.shape[2]
    parent_rows = parent.shape[0]
    chunks = rbuf.shape[0]
    bufs = [rbuf.at[c] for c in range(chunks)] + [sbuf.at[c] for c in range(chunks)]
    sends = []

    def wide_of(off):
        return ((z + off[1] + 4) % 4) * 4 + (y + off[0] + 4) % 4

    def vec(axis, k):
        return (k, 0) if axis == 0 else (0, k)

    def add(p, q):
        return (p[0] + q[0], p[1] + q[1])

    def region(g, off, h, q=None):
        start = wide_of(off) * pb + h * half + (0 if q is None else q * quarter)
        size = half if q is None else quarter
        return bufs[g].at[pl.ds(pl.multiple_of(start, quarter), size)]

    def gcopy(g, axis, s, msg, ref):
        i = (axis * 2 + (0 if s == PLUS else 1)) * PER_LINK + msg
        return pltpu.make_async_remote_copy(
            src_ref=ref, dst_ref=ref, send_sem=g_send.at[g, i], recv_sem=g_recv.at[g, i],
            device_id=(f, wide_of(vec(axis, s))), device_id_type=MESH,
        )

    def gsend(g, axis, s, msg, ref):
        copy = gcopy(g, axis, s, msg, ref)
        copy.start()
        sends.append(copy)

    def gwait(g, axis, s, msg, ref):
        gcopy(g, axis, s, msg, ref).wait_recv()

    def quart(s):
        return 0 if s == PLUS else 1

    here = (0, 0)

    def g_own(g):
        for axis, s in DIRS:
            gsend(g, axis, s, D1, region(g, here, axis))
        for axis, s in DIRS:
            gsend(g, axis, s, OWN, region(g, here, 1 - axis))

    def g_d1(g):
        def near(axis, s):
            for t in (PLUS, MINUS):
                gsend(g, 1 - axis, t, NEAR_M if s == PLUS else NEAR_P, region(g, vec(axis, -s), axis))

        for axis, s in DIRS:
            off = vec(axis, -s)
            gwait(g, axis, s, D1, region(g, off, axis))
            gsend(g, axis, s, R1, region(g, off, axis, quart(s)))
        for axis, s in DIRS:
            near(axis, s)

    def g_r1(g):
        for axis, s in DIRS:
            ref = region(g, vec(axis, 2), axis, quart(s))
            gwait(g, axis, s, R1, ref)
            for t in (PLUS, MINUS):
                gsend(g, 1 - axis, t, OPP_A if s == PLUS else OPP_B, ref)

    def g_d2own(g):
        for axis, s in DIRS:
            off = vec(axis, -s)
            gwait(g, axis, s, OWN, region(g, off, 1 - axis))
            gsend(g, axis, s, R_OWN, region(g, off, 1 - axis, quart(s)))

    def g_d2near(g):
        for j, msg, relay in ((MINUS, NEAR_M, R_NEAR_M), (PLUS, NEAR_P, R_NEAR_P)):
            for axis, s in DIRS:
                off = add(vec(axis, -s), vec(1 - axis, j))
                gwait(g, axis, s, msg, region(g, off, 1 - axis))
                gsend(g, axis, s, relay, region(g, off, 1 - axis, quart(s)))

    def g_d2opp(g):
        for axis, s in DIRS:
            off = add(vec(axis, -s), vec(1 - axis, 2))
            for q, msg in ((0, OPP_A), (1, OPP_B)):
                ref = region(g, off, 1 - axis, q)
                gwait(g, axis, s, msg, ref)
                if q == quart(s):
                    gsend(g, axis, s, R_OPP, ref)

    def g_r2(g, msg, j):
        for axis, s in DIRS:
            off = add(vec(axis, 2), vec(1 - axis, j))
            gwait(g, axis, s, msg, region(g, off, 1 - axis, quart(s)))

    def g_r2all(g):
        for msg, j in ((R_OWN, 0), (R_NEAR_M, MINUS), (R_NEAR_P, PLUS), (R_OPP, 2)):
            g_r2(g, msg, j)

    barrier = pltpu.get_barrier_semaphore()
    for axis, s in DIRS:
        pl.semaphore_signal(barrier, inc=1, device_id=(f, wide_of(vec(axis, s))), device_id_type=MESH)
    for d in range(1, 8):
        pl.semaphore_signal(barrier, inc=1, device_id=((f + d) % 8, w), device_id_type=MESH)

    own = pl.ds(pl.multiple_of(w * pb, pb), pb)
    loads = []
    for c in range(chunks):
        cols = pl.ds(c * CHUNK, CHUNK)
        loads.append(pltpu.make_async_copy(rhs_hbm.at[:, cols], rbuf.at[c, own], loc.at[c]))
    smalls = [
        pltpu.make_async_copy(rows_hbm, rows_ref, loc.at[chunks + 3]),
        pltpu.make_async_copy(owner_hbm, owner_ref, loc.at[chunks + 4]),
        pltpu.make_async_copy(count_hbm, count_ref, loc.at[chunks + 5]),
    ]
    loads.append(pltpu.make_async_copy(inv_hbm, inv, loc.at[chunks]))
    loads.append(pltpu.make_async_copy(below_hbm, below, loc.at[chunks + 1]))
    loads.append(pltpu.make_async_copy(parent_hbm, parent, loc.at[chunks + 2]))
    for copy in loads[:chunks] + smalls + loads[chunks:]:
        copy.start()

    pl.semaphore_wait(barrier, 11)

    loads[0].wait()
    g_own(0)
    loads[1].wait()
    g_own(1)

    def alive(j):
        return w * tiles + j < count_ref[f]

    def slots_of_tiles():
        for copy in smalls:
            copy.wait()
        none = jnp.full((1, height), parent_rows, jnp.int32)
        rows_out[...] = jnp.full(rows_out.shape, parent_rows, jnp.int32)
        for g in range(8):
            index = [jnp.int32(0)] * slots
            found = [jnp.int32(0)] * slots
            seen = jnp.int32(0)
            for j in range(tiles):
                hit = owner_ref[j] == g
                for k in range(slots):
                    this = jnp.logical_and(hit, seen == k)
                    index[k] = jnp.where(this, j, index[k])
                    found[k] = jnp.where(jnp.logical_and(this, alive(j)), 1, found[k])
                seen = seen + jnp.where(hit, 1, 0)
            for k in range(slots):
                slot_idx[g * slots + k] = index[k]
                rows_out[g, k:k + 1, :] = jnp.where(found[k] == 1, rows_ref[index[k]], none)
        rows_in[f] = rows_out[f]
        for d in range(1, 8):
            to = (f + d) % 8
            copy = pltpu.make_async_remote_copy(
                src_ref=rows_out.at[to], dst_ref=rows_in.at[f], send_sem=r_send.at[d], recv_sem=r_recv.at[d],
                device_id=(to, w), device_id_type=MESH,
            )
            copy.start()
            sends.append(copy)

    def wait_rows():
        for d in range(1, 8):
            pltpu.make_async_remote_copy(
                src_ref=rows_in.at[(f + 8 - d) % 8], dst_ref=rows_in.at[(f + 8 - d) % 8],
                send_sem=r_send.at[d], recv_sem=r_recv.at[d], device_id=((f + d) % 8, w), device_id_type=MESH,
            ).wait_recv()

    def build_hits():
        position = lax.broadcasted_iota(jnp.int32, (parent_rows, height), 0)

        def one(i, carry):
            for k in range(slots):
                row = rows_in[i, k:k + 1, :]
                at = pl.ds(pl.multiple_of((i * slots + k) * height, height), height)
                hits[:, at] = jnp.where(position == row, 1.0, 0.0).astype(jnp.bfloat16)
            return carry

        lax.fori_loop(0, 8, one, 0)

    def block(ref, acc, src, k):
        at = pl.ds(pl.multiple_of(k * pb, pb), pb)
        acc[...] += jnp.dot(ref[:, at], src[at, :], preferred_element_type=jnp.float32)

    def mm(ref, acc, src, lo, hi, place=lambda i: i):
        def step(i, carry):
            block(ref, acc, src, place(i))
            return carry

        lax.fori_loop(lo, hi, step, 0)

    def xcopy(c, sid, rid, src, dst, to):
        return pltpu.make_async_remote_copy(
            src_ref=src, dst_ref=dst, send_sem=x_send.at[c, sid], recv_sem=x_recv.at[c, rid],
            device_id=(to, w), device_id_type=MESH,
        )

    def xstart(*args):
        copy = xcopy(*args)
        copy.start()
        sends.append(copy)

    def chip_at(k):
        return (chip + k + 4) % 4

    def pack(c):
        for j in range(tiles):
            value = u_acc[j * height:(j + 1) * height, :]
            u_tiles[j] = jnp.where(alive(j), value, jnp.zeros_like(value)).astype(jnp.bfloat16)

    def pack_for(c, to):
        for k in range(slots):
            packed[c, to, k] = u_tiles[slot_idx[to * slots + k]]

    def xsend(c):
        steps = [(chip_at(2) * 2 + c2, 5 + c2, 5 + core) for c2 in range(2)]
        for n, s in enumerate((PLUS, MINUS)):
            steps += [(chip_at(s) * 2 + c2, 1 + n * 2 + c2, 1 + n * 2 + core) for c2 in range(2)]
        steps.append((chip * 2 + 1 - core, 0, 0))
        pack_for(c, steps[0][0])
        for i, (to, sid, rid) in enumerate(steps):
            if i + 1 < len(steps):
                pack_for(c, steps[i + 1][0])
            else:
                for k in range(slots):
                    arrived[c, f, k] = u_tiles[slot_idx[f * slots + k]]
            xstart(c, sid, rid, packed.at[c, to], arrived.at[c, f], to)

    def add_chip(c, k):
        other = chip * 2 + 1 - core
        if k == 0:
            ref = arrived.at[c, other]
            xcopy(c, 0, 0, ref, ref, other).wait_recv()
        else:
            first = {-1: 1, 1: 3, 2: 5}[k]
            for c2 in range(2):
                ref = arrived.at[c, chip_at(k) * 2 + c2]
                xcopy(c, 0, first + c2, ref, ref, other).wait_recv()
        cols = slice(c * CHUNK, (c + 1) * CHUNK)
        per = 2 * slots * height
        values = arrived[c, pl.ds(chip_at(k) * 2, 2)].reshape(per, CHUNK)
        at = pl.ds(pl.multiple_of(chip_at(k) * per, per), per)
        before = parent[:, cols].astype(jnp.float32) if k == 0 else parent_out[:, cols]
        parent_out[:, cols] = before - jnp.dot(hits[:, at], values, preferred_element_type=jnp.float32)

    def sign(i):
        return 2 * (i % 2) - 1

    def at_near(i):
        return wide_of((sign(i) * (1 - i // 2), sign(i) * (i // 2)))

    def at_diagonal(i):
        return wide_of((sign(i), 2 * (i // 2) - 1))

    def at_far(i):
        return wide_of((2 * i, 2 - 2 * i))

    def at_farther(i, j):
        return wide_of((2 * (1 - i) + j * i, j * (1 - i) + 2 * i))

    sides = [(inv, s_acc)] * chunks + [(below, u_acc)] * chunks

    def take(g, count, place):
        mm(sides[g][0], sides[g][1], bufs[g], 0, count, place)

    def take_own(g):
        acc = sides[g][1]
        acc[...] = jnp.zeros_like(acc)
        take(g, 1, lambda i: w)

    def late_first(g):
        g_r2(g, R_OWN, 0)
        take(g, 2, at_far)

    def late_last(g):
        g_r2(g, R_NEAR_M, MINUS)
        take(g, 2, lambda i: at_farther(i, MINUS))
        g_r2(g, R_NEAR_P, PLUS)
        take(g, 2, lambda i: at_farther(i, PLUS))
        g_r2(g, R_OPP, 2)
        take(g, 1, lambda i: wide_of((2, 2)))

    def store_solved(c):
        value = s_acc[...].astype(jnp.bfloat16)
        sbuf[c, own, :] = value
        solved_out[:, c * CHUNK:(c + 1) * CHUNK] = value

    slots_of_tiles()
    g_d1(0)
    g_r1(0)
    loads[2].wait()
    take_own(0)
    g_d2own(0)
    take(0, 4, at_near)
    g_d2near(0)
    g_d1(1)
    take(0, 4, at_diagonal)
    g_d2opp(0)
    wait_rows()
    build_hits()
    g_r1(1)
    late_first(0)
    g_d2own(1)
    late_last(0)
    store_solved(0)
    take_own(1)
    g_own(2)
    take(1, 4, at_near)
    g_d2near(1)
    g_d1(2)
    take(1, 4, at_diagonal)
    g_d2opp(1)
    g_r1(2)
    late_first(1)
    g_d2own(2)
    late_last(1)
    store_solved(1)
    loads[3].wait()
    take_own(2)
    g_own(3)
    g_d2near(2)
    take(2, 4, at_near)
    g_d2opp(2)
    g_d1(3)
    take(2, 4, at_diagonal)
    late_first(2)
    g_r1(3)
    g_d2own(3)
    late_last(2)
    pack(0)
    xsend(0)
    g_d2near(3)
    take_own(3)
    take(3, 4, at_near)
    g_d2opp(3)
    take(3, 4, at_diagonal)
    late_first(3)
    late_last(3)
    pack(1)
    xsend(1)
    loads[4].wait()
    for k in (0, -1, 1, 2):
        add_chip(0, k)
    for k in (0, -1, 1, 2):
        add_chip(1, k)
    for copy in sends:
        copy.wait_send()


def write_kernel(solved_in, parent_in, solved_hbm, parent_hbm, sem):
    copies = [
        pltpu.make_async_copy(solved_in, solved_hbm, sem.at[0]),
        pltpu.make_async_copy(parent_in, parent_hbm, sem.at[1]),
    ]
    for copy in copies:
        copy.start()
    for copy in copies:
        copy.wait()


def call(inv, below, rhs, parent_rhs, tile_rows, owners, tile_count):
    rows, pivots = inv.shape
    under = below.shape[0]
    width = rhs.shape[1]
    chunks = width // CHUNK
    tiles, _, height = tile_rows.shape
    slots = 2
    parent_rows = parent_rhs.shape[0]
    bf, f32 = jnp.bfloat16, jnp.float32
    anyspace = pl.BlockSpec(memory_space=pl.ANY)
    hbm = pl.BlockSpec(memory_space=pltpu.HBM)
    vmem = pl.BlockSpec(memory_space=pltpu.VMEM)
    dma = pltpu.SemaphoreType.DMA
    solved, parent_new = pl.pallas_call(
        kernel,
        out_shape=(
            pltpu.VMEM((rows, width), bf),
            pltpu.VMEM((parent_rows, width), f32),
        ),
        in_specs=[hbm] * 7,
        out_specs=(vmem, vmem),
        scratch_shapes=[
            pltpu.VMEM((rows, pivots), bf),
            pltpu.VMEM((under, pivots), bf),
            pltpu.VMEM((chunks, pivots, CHUNK), bf),
            pltpu.VMEM((chunks, pivots, CHUNK), bf),
            pltpu.VMEM((rows, CHUNK), f32),
            pltpu.VMEM((under, CHUNK), f32),
            pltpu.VMEM((tiles, height, CHUNK), bf),
            pltpu.SMEM((8 * slots,), jnp.int32),
            pltpu.VMEM((8, 8, height), jnp.int32),
            pltpu.VMEM((8, 8, height), jnp.int32),
            pltpu.VMEM((chunks, 8, slots, height, CHUNK), bf),
            pltpu.VMEM((chunks, 8, slots, height, CHUNK), bf),
            pltpu.VMEM((parent_rows, 8 * slots * height), bf),
            pltpu.VMEM((parent_rows, width), bf),
            pltpu.VMEM(tile_rows.shape, jnp.int32),
            pltpu.SMEM(owners.shape, jnp.int32),
            pltpu.SMEM(tile_count.shape, jnp.int32),
            dma((2 * chunks, 4 * PER_LINK)),
            dma((2 * chunks, 4 * PER_LINK)),
            dma((chunks, 7)),
            dma((chunks, 7)),
            dma((8,)),
            dma((8,)),
            dma((chunks + 6,)),
        ],
        compiler_params=pltpu.CompilerParams(
            collective_id=0, has_side_effects=True, vmem_limit_bytes=60 * 1024 * 1024
        ),
        name="solve_extend_add",
    )(inv, below, rhs, parent_rhs, tile_rows, owners, tile_count)
    return pl.pallas_call(
        write_kernel,
        out_shape=(
            jax.ShapeDtypeStruct((rows, width), bf),
            jax.ShapeDtypeStruct((parent_rows, width), f32),
        ),
        in_specs=[anyspace] * 2,
        out_specs=(anyspace, anyspace),
        scratch_shapes=[dma((2,))],
        compiler_params=pltpu.CompilerParams(vmem_limit_bytes=1024 * 1024),
        name="write",
    )(solved, parent_new)


def body(inv_diag, below, rhs, tile_count, tile_owner, tile_rows, parent_rhs):
    solved, parent_new = call(
        inv_diag[0], below[0], rhs[0], parent_rhs[0], tile_rows.transpose(1, 0, 2), tile_owner[0, :, 0], tile_count
    )
    return solved[None], parent_new[None]


def solution(mesh):
    spec = P("front", "wide", None)
    return jax.shard_map(
        body,
        mesh=mesh,
        in_specs=(spec, spec, spec, P(), spec, spec, spec),
        out_specs=(spec, spec),
        check_vma=False,
    )
```
